128 devices in a mesh: blk: 32 (over x, z_hi, y), org: 4 (over z_lo, core).
Axes of the slice: x: 4, y: 4, z: 4 (z_hi: 2, z_lo: 2; z = z_hi * 2 + z_lo), core: 2. Of those that a mesh axis runs over, the one named last changes fastest.
Arguments:
- warm_labels: float32 [256, 512, 1024], P('blk', None, 'org'), may hold values from 0 to 6
- link_costs: float32 [4, 256, 512], P(None, 'blk'), may hold values from 0.05 to 1.5
- anchor_nodes: int32 [1024], P('org'), may hold values from 0 to 131071
- demand: float32 [1024], P('org'), may hold values from 0.2 to 2
Outputs:
- labels: float32 [256, 512, 1024], P('blk', None, 'org')
- link_weights: float32 [4, 256, 512], P(None, 'blk', 'org')
The draws below stay inside these ranges and needn't reach their ends.
Inputs may be any that keep to these rules, and one draw needn't show every extreme that they name: `anchor_nodes`: node numbers r * 512 + c.
All inputs are finite; a program needn't handle non-finite values.
Results may differ from the reference program's by a relative error of at most 0.0003.
Values sent between devices are 32-bit elements; how exact they have to be, the bound alone decides.
No kernel may reach another device: no remote copies, remote signals or barrier semaphores. Data moves between devices by JAX's collectives and lax.ppermute only.
A program may use at most 128 MiB of HBM per device.

```python
import math
import jax
import jax.numpy as jnp
from jax import lax

ROWS_DEV = 8
GCOLS = 512
ANCHORS = 1024
INNER = 2
ROUNDS = 3
NROWS = 256
NODES = 131072
N_BLK = 32


def place_ends(array, stream_key, smallest, high):
    longest = array.shape.index(max(array.shape))
    spots = []
    for shift in (0, 1):
        where = [jax.random.randint(jax.random.fold_in(stream_key, axis), (), 0, length) for axis, length in enumerate(array.shape)]
        where[longest] = (where[longest] + shift) % array.shape[longest]
        spots.append(tuple(where))
    return array.at[spots[0]].set(smallest).at[spots[1]].set(high)


def block_scale(rng, extent, cuts, smallest, top_value):
    level = 1.0
    for position, blocks in cuts:
        steps = jax.random.uniform(jax.random.fold_in(jax.random.fold_in(rng, 6), position), (blocks,), jnp.float32, smallest / len(cuts), top_value / len(cuts))
        level = level * jnp.repeat(jnp.exp(steps), extent[position] // blocks).reshape((-1,) + (1,) * (len(extent) - 1 - position))
    return level


def setup_inputs(seed: int = 0) -> dict:
    key_list = jax.random.split(jax.random.key(seed), 5)
    warm_labels = jnp.clip(6.0 * jax.random.uniform(key_list[0], (NROWS, GCOLS, ANCHORS), jnp.float32) ** block_scale(key_list[0], (NROWS, GCOLS, ANCHORS), ((0, 32), (2, 4)), -0.2, 0.2), 0.0, 6.0)
    link_costs = jnp.clip(jnp.exp(math.log(1.5) - 3.4011974 * jax.random.uniform(key_list[1], (4, NROWS, GCOLS), jnp.float32) ** block_scale(key_list[1], (4, NROWS, GCOLS), ((1, 32),), -0.2, 0.2)), 0.05, 1.5)
    anchor_nodes = place_ends(jax.random.randint(key_list[2], (ANCHORS,), 0, NODES), jax.random.fold_in(key_list[2], 1), 0, NODES - 1).astype(jnp.int32)
    demand = jnp.clip(jnp.exp(math.log(2.0) - 2.3025851 * jax.random.uniform(key_list[3], (ANCHORS,), jnp.float32) ** block_scale(key_list[3], (ANCHORS,), ((0, 4),), -0.2, 0.2)), 0.2, 2.0)
    return dict(warm_labels=warm_labels, link_costs=link_costs, anchor_nodes=anchor_nodes, demand=demand)


far_value = 1e9
temper = 0.5


def relax_step(padded, costs):
    centre = padded[1:-1]
    edge = jnp.full((centre.shape[0], 1, centre.shape[2]), far_value, centre.dtype)
    west = jnp.concatenate([edge, centre[:, :-1]], axis=1) + costs[0, 1:-1][:, :, None]
    east = jnp.concatenate([centre[:, 1:], edge], axis=1) + costs[1, 1:-1][:, :, None]
    north = padded[:-2] + costs[2, 1:-1][:, :, None]
    south = padded[2:] + costs[3, 1:-1][:, :, None]
    return jnp.minimum(jnp.minimum(jnp.minimum(centre, west), jnp.minimum(east, north)), south)


def link_terms(padded, labels, costs, weights):
    edge = jnp.full((labels.shape[0], 1, labels.shape[2]), far_value, labels.dtype)
    sides = (jnp.concatenate([edge, labels[:, :-1]], axis=1),
             jnp.concatenate([labels[:, 1:], edge], axis=1),
             padded[:-2], padded[2:])
    result = []
    for side in range(4):
        expo = jnp.exp(-temper * (sides[side] + costs[side][:, :, None] - labels))
        result.append(jnp.einsum("rco,o->rc", expo, weights, precision=lax.Precision.HIGHEST))
    return jnp.stack(result)


def reference(warm_labels, link_costs, anchor_nodes, demand):
    total_rows = ROWS_DEV * N_BLK
    node_ids = (jnp.arange(total_rows, dtype=jnp.int32)[:, None] * GCOLS
                + jnp.arange(GCOLS, dtype=jnp.int32)[None, :]).astype(jnp.int32)
    block = 128 if ANCHORS % 128 == 0 else ANCHORS
    blocks = ANCHORS // block
    warm_blocks = warm_labels.reshape(total_rows, GCOLS, blocks, block).transpose(2, 0, 1, 3)
    cost_pad = jnp.pad(link_costs, ((0, 0), (1, 1), (0, 0)))

    def one_block(packed):
        warm, anchors, weights = packed
        labels = jnp.where(node_ids[:, :, None] == anchors[None, None, :], jnp.zeros_like(warm), warm)
        for sweep in range(ROUNDS * INNER):
            padded = jnp.pad(labels, ((1, 1), (0, 0), (0, 0)), constant_values=far_value)
            labels = relax_step(padded, cost_pad)
        padded = jnp.pad(labels, ((1, 1), (0, 0), (0, 0)), constant_values=far_value)
        return labels, link_terms(padded, labels, link_costs, weights)

    label_blocks, partials = lax.map(one_block, (warm_blocks, anchor_nodes.reshape(blocks, block),
                                                 demand.reshape(blocks, block)))
    labels = label_blocks.transpose(1, 2, 0, 3).reshape(total_rows, GCOLS, ANCHORS)
    link_weights = jnp.sum(partials, axis=0) / ANCHORS
    return labels, link_weights
```

```python
import functools
import jax
import jax.numpy as jnp
from jax import lax
from jax.experimental import pallas as pl
from jax.experimental.pallas import tpu as pltpu
from jax.sharding import PartitionSpec as P

ANCHORS = 1024
STEPS = 6
EDGE = 6
FIRST = 4
PAD = 8
CH = 128
far_value = 1000000000.0
temper = 0.5
F32 = jnp.float32
WEST, EAST, NORTH, SOUTH = range(4)
OUTER = (NORTH, SOUTH)
INNER_SIDE = (SOUTH, NORTH)


def row_of(side, depth):
    return depth if side == 0 else 7 - depth


def cost_row(side, depth):
    return EDGE + row_of(side, depth)


def chunks(cols, body):
    def step(i, carry):
        body(pl.multiple_of(i * CH, CH))
        return carry

    lax.fori_loop(0, cols // CH, step, 0)


def halves(body):
    def step(h, carry):
        body(h, pl.ds(pl.multiple_of(h * 128, 128), 128))
        return carry

    lax.fori_loop(0, 2, step, 0)


def clear_pads(buf, rows, cols):
    zero = jnp.zeros((PAD, 128), F32)
    for r in range(rows):
        buf[r, pl.ds(0, PAD), :] = zero
        buf[r, pl.ds(cols + PAD, PAD), :] = zero


def anchored(values, anchors, node0):
    ids = node0 + lax.broadcasted_iota(jnp.int32, values.shape, 0)
    return jnp.where(ids == anchors, 0.0, values)


def add_lane_sum(sums, side, row, piece, terms):
    at = side * 8 + row
    sums[piece, at : at + 1, :] += jnp.sum(terms, axis=1)[None, :]


def spread_kernel(lanes, cols_ref, out_ref, sem):
    cols = cols_ref.shape[0]

    def body(c0):
        block = cols_ref[pl.ds(c0, CH), :]
        for lane in range(lanes):
            out_ref[lane, pl.ds(c0, CH), :] = jnp.broadcast_to(block[:, lane : lane + 1], (CH, 128))

    chunks(cols, body)


def first_kernel(row0, own, north, south, anchors, demand, cost, g_out, d_out, lab_out, sums, labels, bufa, bufb, ebuf, sem):
    cols = own.shape[1]
    rows = 8 + 2 * FIRST
    bufs = (bufa, bufb)
    sums[...] = jnp.zeros(sums.shape, F32)

    clear_pads(bufa, rows, cols)
    clear_pads(bufb, rows, cols)
    clear_pads(ebuf, 4, cols)

    def loads(h):
        return [
            pltpu.make_async_copy(
                ref.at[i, :, pl.ds(h * 128, 128)], bufs[h].at[at + i, pl.ds(PAD, cols), :], sem.at[at + i]
            )
            for ref, count, at in ((north, FIRST, 0), (own, 8, FIRST), (south, FIRST, FIRST + 8))
            for i in range(count)
        ]

    for copy in loads(0):
        copy.start()
    for h in range(2):
        lanes = pl.ds(h * 128, 128)
        anc = anchors[:, lanes]
        dem = demand[:, lanes]
        level = (bufs[h], bufs[1 - h])
        for copy in loads(h):
            copy.wait()

        def mark(i, carry, buf=level[0], anc=anc):
            node0 = (row0[0] + i - FIRST) * cols

            def body(c0):
                here = pl.ds(c0 + PAD, CH)
                buf[i, here, :] = anchored(buf[i, here, :], anc, node0 + c0)

            chunks(cols, body)
            return carry

        lax.fori_loop(0, rows, mark, 0)
        for t in range(1, STEPS + 1):
            src, dst = level[(t - 1) % 2], level[t % 2]
            for side in range(2):
                at = t - 1 if side == 0 else rows - t
                inner = t if side == 0 else rows - 1 - t
                j = row_of(side, t - FIRST - 1) + EDGE

                def edge(c0, side=side, at=at, inner=inner, j=j, t=t, src=src, h=h):
                    centre = src[at, pl.ds(c0 + PAD, CH), :]
                    west = src[at, pl.ds(c0 + PAD - 1, CH), :] + cost[4 * j + WEST, pl.ds(c0, CH), :]
                    east = src[at, pl.ds(c0 + PAD + 1, CH), :] + cost[4 * j + EAST, pl.ds(c0, CH), :]
                    within = src[inner, pl.ds(c0 + PAD, CH), :] + cost[4 * j + INNER_SIDE[side], pl.ds(c0, CH), :]
                    g_out[side * STEPS + t - 1, h, pl.ds(c0, CH), :] = jnp.minimum(
                        jnp.minimum(centre, west), jnp.minimum(east, within)
                    )
                    d_out[side * STEPS + t - 1, h, pl.ds(c0, CH), :] = centre

                chunks(cols, edge)

            def row(i, carry, src=src, dst=dst):
                j = 4 * (i - FIRST + EDGE)

                def body(c0):
                    here = pl.ds(c0, CH)
                    centre = src[i, pl.ds(c0 + PAD, CH), :]
                    west = src[i, pl.ds(c0 + PAD - 1, CH), :] + cost[j + WEST, here, :]
                    east = src[i, pl.ds(c0 + PAD + 1, CH), :] + cost[j + EAST, here, :]
                    up = src[i - 1, pl.ds(c0 + PAD, CH), :] + cost[j + NORTH, here, :]
                    down = src[i + 1, pl.ds(c0 + PAD, CH), :] + cost[j + SOUTH, here, :]
                    dst[i, pl.ds(c0 + PAD, CH), :] = jnp.minimum(
                        jnp.minimum(jnp.minimum(centre, west), jnp.minimum(east, up)), down
                    )

                chunks(cols, body)
                return carry

            lax.fori_loop(t, rows - t, row, 0)

        if h == 0:
            for copy in loads(1):
                copy.start()

        def final(c0, buf=level[0], lanes=lanes):
            for r in range(4):
                value = buf[r + STEPS, pl.ds(c0 + PAD, CH), :]
                lab_out[r, pl.ds(c0, CH), lanes] = value
                ebuf[r, pl.ds(c0 + PAD, CH), :] = jnp.exp(-temper * value)

        chunks(cols, final)

        def link(c0, buf=level[0], dem=dem):
            piece = c0 // CH
            for r in range(4):
                inv = dem * jnp.exp(temper * buf[r + STEPS, pl.ds(c0 + PAD, CH), :])
                add_lane_sum(sums, WEST, r + 2, piece, inv * ebuf[r, pl.ds(c0 + PAD - 1, CH), :])
                add_lane_sum(sums, EAST, r + 2, piece, inv * ebuf[r, pl.ds(c0 + PAD + 1, CH), :])
                if r > 0:
                    add_lane_sum(sums, NORTH, r + 2, piece, inv * ebuf[r - 1, pl.ds(c0 + PAD, CH), :])
                if r < 3:
                    add_lane_sum(sums, SOUTH, r + 2, piece, inv * ebuf[r + 1, pl.ds(c0 + PAD, CH), :])

        chunks(cols, link)

    put_rows([(lab_out.at[r], labels.at[r + 2]) for r in range(4)], sem)


def put_rows(pairs, sem):
    copies = [pltpu.make_async_copy(src, dst, sem.at[n]) for n, (src, dst) in enumerate(pairs)]
    for copy in copies:
        copy.start()
    for copy in copies:
        copy.wait()


def next_kernel(depth, last, *refs):
    row0, north, south, anchors, demand, cost, g_in, d_in, in_lab, sums_in, _ = refs[:11]
    if last:
        far_out, lab_out, sums, labels, dbuf, ebuf, gbuf, sem = refs[11:]
    else:
        g_out, d_out, lab_out, sums, labels, dbuf, ebuf, sem = refs[11:]
    cols = north.shape[1]
    at_rows = tuple(row_of(side, STEPS - depth) for side in range(2))
    sums[...] = sums_in[...]

    def half(h, lanes):
        anc = anchors[:, lanes]
        dem = demand[:, lanes]
        clear_pads(dbuf, STEPS, cols)
        clear_pads(ebuf, 1, cols)
        for side in range(2):
            halo = (north, south)[side]
            within = 0 if side == 0 else in_lab.shape[0] - 1
            node0 = (row0[0] + row_of(side, -depth)) * cols

            def chain(c0, side=side, halo=halo, node0=node0):
                here = pl.ds(c0, CH)
                value = anchored(halo[0, here, lanes], anc, node0 + c0)
                dbuf[0, pl.ds(c0 + PAD, CH), :] = value
                for t in range(1, STEPS + 1):
                    j = 4 * cost_row(side, t - depth)
                    value = jnp.minimum(g_in[side * STEPS + t - 1, h, here, :], value + cost[j + OUTER[side], here, :])
                    if t < STEPS:
                        dbuf[t, pl.ds(c0 + PAD, CH), :] = value
                lab_out[side, here, lanes] = value
                ebuf[0, pl.ds(c0 + PAD, CH), :] = jnp.exp(-temper * value)

            chunks(cols, chain)

            for t in range(1, STEPS + 1):
                j = 4 * cost_row(side, t - depth - 1)

                def ahead(c0, side=side, t=t, j=j):
                    here = pl.ds(c0, CH)
                    centre = dbuf[t - 1, pl.ds(c0 + PAD, CH), :]
                    west = dbuf[t - 1, pl.ds(c0 + PAD - 1, CH), :] + cost[j + WEST, here, :]
                    east = dbuf[t - 1, pl.ds(c0 + PAD + 1, CH), :] + cost[j + EAST, here, :]
                    within = d_in[side * STEPS + t - 1, h, here, :] + cost[j + INNER_SIDE[side], here, :]
                    best = jnp.minimum(jnp.minimum(centre, west), jnp.minimum(east, within))
                    if not last:
                        g_out[side * STEPS + t - 1, h, here, :] = best
                        d_out[side * STEPS + t - 1, h, here, :] = centre
                    else:
                        if t > 1:
                            best = jnp.minimum(best, gbuf[here, :] + cost[j + OUTER[side], here, :])
                        if t < STEPS:
                            gbuf[here, :] = best
                        else:
                            far_out[side, h, here, :] = best

                chunks(cols, ahead)

            def link(c0, side=side, within=within):
                here = pl.ds(c0, CH)
                piece = c0 // CH
                at = at_rows[side]
                inside = row_of(side, STEPS - depth + 1)
                inv = dem * jnp.exp(temper * lab_out[side, here, lanes])
                other = in_lab[within, here, lanes]
                add_lane_sum(sums, WEST, at, piece, inv * ebuf[0, pl.ds(c0 + PAD - 1, CH), :])
                add_lane_sum(sums, EAST, at, piece, inv * ebuf[0, pl.ds(c0 + PAD + 1, CH), :])
                add_lane_sum(sums, INNER_SIDE[side], at, piece, inv * jnp.exp(-temper * other))
                inv_in = dem * jnp.exp(temper * other)
                add_lane_sum(sums, OUTER[side], inside, piece, inv_in * ebuf[0, pl.ds(c0 + PAD, CH), :])

            chunks(cols, link)

    halves(half)
    put_rows([(lab_out.at[side], labels.at[at_rows[side]]) for side in range(2)], sem)


def cross_kernel(depth, row0, north, south, anchors, demand, path, far_in, lab, sums_in, sums, sem):
    cols = north.shape[1]
    sums[...] = sums_in[...]

    def half(h, lanes):
        anc = anchors[:, lanes]
        dem = demand[:, lanes]

        def body(c0):
            here = pl.ds(c0, CH)
            for side in range(2):
                halo = (north, south)[side]
                node0 = (row0[0] + row_of(side, -depth)) * cols
                value = anchored(halo[0, here, lanes], anc, node0 + c0) + path[side, here, :]
                value = jnp.minimum(value, far_in[side, h, here, :])
                part = dem * jnp.exp(temper * lab[side, here, lanes]) * jnp.exp(-temper * value)
                add_lane_sum(sums, OUTER[side], row_of(side, 0), c0 // CH, part)

        chunks(cols, body)

    halves(half)


VM = pl.BlockSpec(memory_space=pltpu.VMEM)
SM = pl.BlockSpec(memory_space=pltpu.SMEM)
HB = pl.BlockSpec(memory_space=pltpu.HBM)


def kernel_call(body, outs, scratch, limit, specs, args, name, aliases=None, sems=4):
    return pl.pallas_call(
        body,
        out_shape=[
            jax.ShapeDtypeStruct(shape, F32) if spec is HB else pltpu.VMEM(shape, F32) for shape, spec in outs
        ],
        in_specs=specs,
        out_specs=[spec for _, spec in outs],
        scratch_shapes=[pltpu.VMEM(s, F32) for s in scratch] + [pltpu.SemaphoreType.DMA((sems,))],
        compiler_params=pltpu.CompilerParams(vmem_limit_bytes=limit),
        cost_estimate=pl.CostEstimate(flops=1 << 20, bytes_accessed=32 << 20, transcendentals=0),
        input_output_aliases=aliases or {},
        name=name,
    )(*(pltpu.with_memory_space_constraint(v, pltpu.HBM) if spec is HB else v for v, spec in zip(args, specs)))


def local(warm, link_costs, anchor_nodes, demand):
    rows, cols, lanes = warm.shape
    count = lax.axis_size("blk")
    me = lax.axis_index("blk")
    up = [(i, i + 1) for i in range(count - 1)]
    down = [(i + 1, i) for i in range(count - 1)]

    def exchange(first, size):
        a = rows - first - size + 1
        north = lax.ppermute(warm[a : a + size], "blk", up)
        south = lax.ppermute(warm[first - 1 : first - 1 + size], "blk", down)
        return north, south

    cost_n = lax.ppermute(link_costs[:, rows - EDGE :], "blk", up)
    cost_s = lax.ppermute(link_costs[:, :EDGE], "blk", down)
    near = exchange(1, FIRST)
    later = [exchange(k, 1) for k in range(FIRST + 1, STEPS + 2)]

    row = me * rows - EDGE + jnp.arange(rows + 2 * EDGE)[:, None]
    col = jnp.arange(cols)[None, :]
    wall = jnp.stack(
        [
            jnp.broadcast_to(col == 0, (rows + 2 * EDGE, cols)),
            jnp.broadcast_to(col == cols - 1, (rows + 2 * EDGE, cols)),
            jnp.broadcast_to(row == 0, (rows + 2 * EDGE, cols)),
            jnp.broadcast_to(row == rows * count - 1, (rows + 2 * EDGE, cols)),
        ]
    )
    costs = jnp.where(wall, far_value, jnp.concatenate([cost_n, link_costs, cost_s], axis=1))
    path = jnp.stack([cost_n[NORTH].sum(axis=0), cost_s[SOUTH].sum(axis=0)])
    flat = jnp.swapaxes(costs, 0, 1).reshape(-1, cols)
    used = flat.shape[0]
    columns = jnp.pad(flat.T, ((0, 0), (0, 128 - used)))
    path_wide = jnp.broadcast_to(path[:, :, None], (2, cols, 128))
    row0 = (me * rows).astype(jnp.int32).reshape(1)
    anc = anchor_nodes.reshape(1, lanes)
    dem = demand.reshape(1, lanes)
    owners = lax.axis_size("org")
    width = cols // owners
    mine = lax.dynamic_slice_in_dim(costs[:, EDGE : EDGE + rows], lax.axis_index("org") * width, width, axis=2)
    scale = jnp.exp(-temper * mine) / ANCHORS
    columns, path_wide, row0, anc, dem, scale = lax.optimization_barrier((columns, path_wide, row0, anc, dem, scale))
    (cost,) = kernel_call(
        functools.partial(spread_kernel, used), [((used, cols, 128), VM)], [], 4 << 20, [VM], (columns,), "spread"
    )
    diag = ((2 * STEPS, 2, cols, 128), VM)
    padded = cols + 2 * PAD
    pieces = ((cols // CH, 4 * rows, CH), VM)
    whole = (warm.shape, HB)
    g, d, lab, sums, labels = kernel_call(
        first_kernel,
        [diag, diag, ((4, cols, lanes), VM), pieces, whole],
        [(rows + 2 * FIRST, padded, 128)] * 2 + [(4, padded, 128)],
        12 << 20, [SM] + [HB] * 3 + [VM] * 3, (row0, warm, near[0], near[1], anc, dem, cost), "first",
        sems=rows + 2 * FIRST,
    )
    g, d, lab, sums, labels = kernel_call(
        functools.partial(next_kernel, FIRST + 1, False),
        [diag, diag, ((2, cols, lanes), VM), pieces, whole],
        [(STEPS, padded, 128), (1, padded, 128)],
        4 << 20, [SM] + [VM] * 9 + [HB], (row0, *later[0], anc, dem, cost, g, d, lab, sums, labels), "second",
        {6: 0, 7: 1, 10: 4},
    )
    far, lab, sums, labels = kernel_call(
        functools.partial(next_kernel, FIRST + 2, True),
        [((2, 2, cols, 128), VM), ((2, cols, lanes), VM), pieces, whole],
        [(STEPS, padded, 128), (1, padded, 128), (cols, 128)],
        4 << 20, [SM] + [VM] * 9 + [HB], (row0, *later[1], anc, dem, cost, g, d, lab, sums, labels), "third", {10: 3},
    )
    (sums,) = kernel_call(
        functools.partial(cross_kernel, FIRST + 3),
        [pieces], [], 4 << 20, [SM] + [VM] * 8,
        (row0, *later[2], anc, dem, path_wide, far, lab, sums), "cross",
    )
    total = lax.all_to_all(sums, "org", split_axis=0, concat_axis=0, tiled=True).sum(axis=0)
    return labels, total.reshape(4, rows, width) * scale


def solution(mesh):
    placed = (P("blk", None, "org"), P(None, "blk", None), P("org"), P("org"))
    return jax.shard_map(
        local,
        mesh=mesh,
        in_specs=placed,
        out_specs=(P("blk", None, "org"), P(None, "blk", "org")),
        check_vma=False,
    )
```

```python
import functools
import jax
import jax.numpy as jnp
from jax import lax
from jax.experimental import pallas as pl
from jax.experimental.pallas import tpu as pltpu
from jax.sharding import PartitionSpec as P


ANCHORS = 1024
STEPS = 6
EDGE = 6
FIRST = 4
PAD = 8
CH = 128
far_value = 1000000000.0
temper = 0.5
F32 = jnp.float32
WEST, EAST, NORTH, SOUTH = range(4)
OUTER = (NORTH, SOUTH)
INNER_SIDE = (SOUTH, NORTH)


def row_of(side, depth):
    return depth if side == 0 else 7 - depth


def cost_row(side, depth):
    return EDGE + row_of(side, depth)


def chunks(cols, body):
    def step(i, carry):
        body(pl.multiple_of(i * CH, CH))
        return carry

    lax.fori_loop(0, cols // CH, step, 0)


def half_lanes(h):
    return pl.ds(h * 128, 128)


def clear_pads(buf, rows, cols):
    zero = jnp.zeros((PAD, 128), F32)
    for r in range(rows):
        for h in range(2):
            buf[r, h, pl.ds(0, PAD), :] = zero
            buf[r, h, pl.ds(cols + PAD, PAD), :] = zero


def anchored(values, anchors, node0):
    ids = node0 + lax.broadcasted_iota(jnp.int32, values.shape, 0)
    return jnp.where(ids == anchors, 0.0, values)


def add_lane_sum(sums, side, row, piece, terms):
    at = side * 8 + row
    sums[piece, at : at + 1, :] += jnp.sum(terms, axis=1)[None, :]


def spread_kernel(lanes, cols_ref, out_ref, sem):
    cols = cols_ref.shape[0]

    def body(c0):
        block = cols_ref[pl.ds(c0, CH), :]
        for lane in range(lanes):
            out_ref[lane, pl.ds(c0, CH), :] = jnp.broadcast_to(block[:, lane : lane + 1], (CH, 128))

    chunks(cols, body)


def first_kernel(info, own, lead1, lead2, more1, more2, anchors, demand, cost, g_out, d_out, lab_out, sums, labels, buf, sem):
    cols = own.shape[1]
    rows = 8 + 2 * FIRST
    odd = info[1]
    north_of = (odd, 1 - odd)
    loads = []
    for i in range(8):
        loads.append((own, i, FIRST + i))
    for lead, more, north in ((lead1, more1, north_of[0]), (lead2, more2, north_of[1])):
        loads.append((lead, None, FIRST + 8 - north * 9))
        for i in range(FIRST - 1):
            loads.append((more, i, (FIRST + 9) * (1 - north) + i))
    loads = [
        pltpu.make_async_copy(
            ref.at[pl.ds(0, cols), half_lanes(h)] if i is None else ref.at[i, :, half_lanes(h)],
            buf.at[at, h, pl.ds(PAD, cols), :],
            sem.at[n, h],
        )
        for n, (ref, i, at) in enumerate(loads)
        for h in range(2)
    ]
    for copy in loads:
        copy.start()
    sums[...] = jnp.zeros(sums.shape, F32)
    clear_pads(buf, rows, cols)
    for copy in loads:
        copy.wait()

    def mark(i, carry):
        node0 = (info[0] + i - FIRST) * cols

        def body(c0):
            here = pl.ds(c0 + PAD, CH)
            for h in range(2):
                buf[i, h, here, :] = anchored(buf[i, h, here, :], anchors[:, half_lanes(h)], node0 + c0)

        chunks(cols, body)
        return carry

    lax.fori_loop(0, rows, mark, 0)
    for t in range(1, STEPS + 1):
        have = rows - 2 * (t - 1)
        for side in range(2):
            at, inner = (0, 1) if side == 0 else (have - 1, have - 2)
            j = 4 * (row_of(side, t - FIRST - 1) + EDGE)

            def edge(c0, side=side, at=at, inner=inner, j=j, t=t):
                here, mid = pl.ds(c0, CH), pl.ds(c0 + PAD, CH)
                west, east, within = (cost[j + k, here, :] for k in (WEST, EAST, INNER_SIDE[side]))
                for h in range(2):
                    centre = buf[at, h, mid, :]
                    g_out[side * STEPS + t - 1, h, here, :] = jnp.minimum(
                        jnp.minimum(centre, buf[at, h, pl.ds(c0 + PAD - 1, CH), :] + west),
                        jnp.minimum(buf[at, h, pl.ds(c0 + PAD + 1, CH), :] + east, buf[inner, h, mid, :] + within),
                    )
                    d_out[side * STEPS + t - 1, h, here, :] = centre

            chunks(cols, edge)

        def row(i, carry, t=t):
            j = 4 * (i + t - FIRST + EDGE)

            def body(c0):
                here, mid = pl.ds(c0, CH), pl.ds(c0 + PAD, CH)
                west, east, up, down = (cost[j + k, here, :] for k in (WEST, EAST, NORTH, SOUTH))
                for h in range(2):
                    buf[i, h, mid, :] = jnp.minimum(
                        jnp.minimum(
                            jnp.minimum(buf[i + 1, h, mid, :], buf[i + 1, h, pl.ds(c0 + PAD - 1, CH), :] + west),
                            jnp.minimum(buf[i + 1, h, pl.ds(c0 + PAD + 1, CH), :] + east, buf[i, h, mid, :] + up),
                        ),
                        buf[i + 2, h, mid, :] + down,
                    )

            chunks(cols, body)
            return carry

        lax.fori_loop(0, have - 2, row, 0)

    stores = [
        pltpu.make_async_copy(buf.at[r, h, pl.ds(PAD, cols), :], labels.at[r + 2, :, half_lanes(h)], sem.at[r, h])
        for r in range(4)
        for h in range(2)
    ]
    for copy in stores:
        copy.start()
    exps = 8

    def final(c0):
        for r in range(4):
            for h in range(2):
                value = buf[r, h, pl.ds(c0 + PAD, CH), :]
                if r % 3 == 0:
                    lab_out[r // 3, pl.ds(c0, CH), half_lanes(h)] = value
                buf[r + exps, h, pl.ds(c0 + PAD, CH), :] = jnp.exp(-temper * value)

    chunks(cols, final)

    def link(c0):
        piece = c0 // CH
        mid = pl.ds(c0 + PAD, CH)
        for r in range(4):
            inv = [demand[:, half_lanes(h)] * jnp.exp(temper * buf[r, h, mid, :]) for h in range(2)]

            def add(side, shift, other, inv=inv, r=r):
                terms = [inv[h] * buf[other + exps, h, pl.ds(c0 + PAD + shift, CH), :] for h in range(2)]
                add_lane_sum(sums, side, r + 2, piece, terms[0] + terms[1])

            add(WEST, -1, r)
            add(EAST, 1, r)
            if r > 0:
                add(NORTH, 0, r - 1)
            if r < 3:
                add(SOUTH, 0, r + 1)

    chunks(cols, link)
    for copy in stores:
        copy.wait()


def pick(got1, got2, odd, side, here, lanes):
    one, two = got1[0, here, lanes], got2[0, here, lanes]
    return jnp.where(odd, one, two) if side == 0 else jnp.where(odd, two, one)


def put_rows(pairs, sem):
    copies = [pltpu.make_async_copy(src, dst, sem.at[n]) for n, (src, dst) in enumerate(pairs)]
    for copy in copies:
        copy.start()
    for copy in copies:
        copy.wait()


def next_kernel(depth, last, *refs):
    info, got1, got2, anchors, demand, cost, g_in, d_in, in_lab, sums_in, _ = refs[:11]
    if last:
        far_out, lab_out, sums, labels, dbuf, ebuf, sem = refs[11:]
    else:
        g_out, d_out, lab_out, sums, labels, dbuf, ebuf, sem = refs[11:]
    cols = got1.shape[1]
    odd = info[1] > 0
    at_rows = tuple(row_of(side, STEPS - depth) for side in range(2))
    sums[...] = sums_in[...]
    clear_pads(dbuf, STEPS, cols)
    clear_pads(ebuf, 1, cols)
    for side in range(2):
        within = 0 if side == 0 else in_lab.shape[0] - 1
        node0 = (info[0] + row_of(side, -depth)) * cols

        def chain(c0, side=side, node0=node0):
            here, mid = pl.ds(c0, CH), pl.ds(c0 + PAD, CH)
            values = []
            for h in range(2):
                values.append(anchored(pick(got1, got2, odd, side, here, half_lanes(h)), anchors[:, half_lanes(h)], node0 + c0))
                dbuf[0, h, mid, :] = values[h]
            for t in range(1, STEPS + 1):
                outer = cost[4 * cost_row(side, t - depth) + OUTER[side], here, :]
                for h in range(2):
                    values[h] = jnp.minimum(g_in[side * STEPS + t - 1, h, here, :], values[h] + outer)
                    if t < STEPS:
                        dbuf[t, h, mid, :] = values[h]
            for h in range(2):
                lab_out[side, here, half_lanes(h)] = values[h]
                ebuf[0, h, mid, :] = jnp.exp(-temper * values[h])

        chunks(cols, chain)

        def ahead(c0, side=side):
            here, mid = pl.ds(c0, CH), pl.ds(c0 + PAD, CH)
            best = [None, None]
            for t in range(1, STEPS + 1):
                j = 4 * cost_row(side, t - depth - 1)
                west, east, inner = (cost[j + k, here, :] for k in (WEST, EAST, INNER_SIDE[side]))
                outer = cost[j + OUTER[side], here, :] if last and t > 1 else None
                for h in range(2):
                    centre = dbuf[t - 1, h, mid, :]
                    found = jnp.minimum(
                        jnp.minimum(centre, dbuf[t - 1, h, pl.ds(c0 + PAD - 1, CH), :] + west),
                        jnp.minimum(
                            dbuf[t - 1, h, pl.ds(c0 + PAD + 1, CH), :] + east,
                            d_in[side * STEPS + t - 1, h, here, :] + inner,
                        ),
                    )
                    if not last:
                        g_out[side * STEPS + t - 1, h, here, :] = found
                        d_out[side * STEPS + t - 1, h, here, :] = centre
                    else:
                        best[h] = found if t == 1 else jnp.minimum(found, best[h] + outer)
            if last:
                for h in range(2):
                    far_out[side, h, here, :] = best[h]

        chunks(cols, ahead)

        def link(c0, side=side, within=within):
            here, mid = pl.ds(c0, CH), pl.ds(c0 + PAD, CH)
            piece = c0 // CH
            at = at_rows[side]
            inside = row_of(side, STEPS - depth + 1)
            terms = [0.0] * 4
            for h in range(2):
                dem = demand[:, half_lanes(h)]
                inv = dem * jnp.exp(temper * lab_out[side, here, half_lanes(h)])
                other = in_lab[within, here, half_lanes(h)]
                terms[0] += inv * ebuf[0, h, pl.ds(c0 + PAD - 1, CH), :]
                terms[1] += inv * ebuf[0, h, pl.ds(c0 + PAD + 1, CH), :]
                terms[2] += inv * jnp.exp(-temper * other)
                terms[3] += dem * jnp.exp(temper * other) * ebuf[0, h, mid, :]
            add_lane_sum(sums, WEST, at, piece, terms[0])
            add_lane_sum(sums, EAST, at, piece, terms[1])
            add_lane_sum(sums, INNER_SIDE[side], at, piece, terms[2])
            add_lane_sum(sums, OUTER[side], inside, piece, terms[3])

        chunks(cols, link)

    put_rows([(lab_out.at[side], labels.at[at_rows[side]]) for side in range(2)], sem)


def cross_kernel(depth, info, got1, got2, anchors, demand, path, far_in, lab, sums_in, sums, sem):
    cols = got1.shape[1]
    odd = info[1] > 0
    sums[...] = sums_in[...]

    def body(c0):
        here = pl.ds(c0, CH)
        for side in range(2):
            node0 = (info[0] + row_of(side, -depth)) * cols
            terms = 0.0
            for h in range(2):
                lanes = half_lanes(h)
                value = pick(got1, got2, odd, side, here, lanes)
                value = anchored(value, anchors[:, lanes], node0 + c0) + path[side, here, :]
                value = jnp.minimum(value, far_in[side, h, here, :])
                terms += demand[:, lanes] * jnp.exp(temper * lab[side, here, lanes]) * jnp.exp(-temper * value)
            add_lane_sum(sums, OUTER[side], row_of(side, 0), c0 // CH, terms)

    chunks(cols, body)


VM = pl.BlockSpec(memory_space=pltpu.VMEM)
SM = pl.BlockSpec(memory_space=pltpu.SMEM)
HB = pl.BlockSpec(memory_space=pltpu.HBM)


def kernel_call(body, outs, scratch, limit, specs, args, aliases=None, sems=(4,)):
    return pl.pallas_call(
        body,
        out_shape=[
            jax.ShapeDtypeStruct(shape, F32) if spec is HB else pltpu.VMEM(shape, F32) for shape, spec in outs
        ],
        in_specs=specs,
        out_specs=[spec for _, spec in outs],
        scratch_shapes=[pltpu.VMEM(s, F32) for s in scratch] + [pltpu.SemaphoreType.DMA(sems)],
        compiler_params=pltpu.CompilerParams(vmem_limit_bytes=limit),
        cost_estimate=pl.CostEstimate(flops=1 << 20, bytes_accessed=32 << 20, transcendentals=0),
        input_output_aliases=aliases or {},
    )(*(pltpu.with_memory_space_constraint(v, pltpu.HBM) if spec is HB else v for v, spec in zip(args, specs)))


def local(warm, link_costs, anchor_nodes, demand):
    rows, cols, lanes = warm.shape
    count = lax.axis_size("blk")
    me = lax.axis_index("blk")
    swaps = [[(i + a, i + 1 - a) for i in range(first, count - 1, 2) for a in (0, 1)] for first in (0, 1)]
    odd = me % 2
    own = warm

    def swap(number, message):
        return lax.ppermute(message, "blk", swaps[number])

    def cut(array, number, first, size, axis):
        low, high = first - 1, rows - first - size + 1
        start = jnp.where(odd == number, high, low)
        return lax.dynamic_slice_in_dim(array, start, size, axis)

    def lead_of(number):
        costs = cut(link_costs, number, 1, EDGE, 1)
        return jnp.concatenate([cut(warm, number, 1, 1, 0)[0], costs.reshape(-1, lanes)])

    lead = [lead_of(number) for number in range(2)]
    got_lead = [swap(number, lead[number]) for number in range(2)]
    warm, lead = lax.optimization_barrier((warm, lead))

    def exchange(first, size):
        return [swap(number, cut(warm, number, first, size, 0)) for number in range(2)]

    near = [*got_lead, *exchange(2, FIRST - 1)]
    later = [exchange(k, 1) for k in range(FIRST + 1, STEPS + 2)]
    got_costs = [m[cols:].reshape(4, EDGE, cols) for m in got_lead]
    cost_n = jnp.where(odd == 1, got_costs[0], got_costs[1])
    cost_s = jnp.where(odd == 1, got_costs[1], got_costs[0])

    row = me * rows - EDGE + jnp.arange(rows + 2 * EDGE)[:, None]
    col = jnp.arange(cols)[None, :]
    wall = jnp.stack(
        [
            jnp.broadcast_to(col == 0, (rows + 2 * EDGE, cols)),
            jnp.broadcast_to(col == cols - 1, (rows + 2 * EDGE, cols)),
            jnp.broadcast_to(row == 0, (rows + 2 * EDGE, cols)),
            jnp.broadcast_to(row == rows * count - 1, (rows + 2 * EDGE, cols)),
        ]
    )
    costs = jnp.where(wall, far_value, jnp.concatenate([cost_n, link_costs, cost_s], axis=1))
    path = jnp.stack([cost_n[NORTH].sum(axis=0), cost_s[SOUTH].sum(axis=0)])
    flat = jnp.swapaxes(costs, 0, 1).reshape(-1, cols)
    used = flat.shape[0]
    columns = jnp.pad(flat.T, ((0, 0), (0, 128 - used)))
    path_wide = jnp.broadcast_to(path[:, :, None], (2, cols, 128))
    info = jnp.stack([me * rows, odd]).astype(jnp.int32)
    anc = anchor_nodes.reshape(1, lanes)
    dem = demand.reshape(1, lanes)
    owners = lax.axis_size("org")
    width = cols // owners
    mine = lax.dynamic_slice_in_dim(costs[:, EDGE : EDGE + rows], lax.axis_index("org") * width, width, axis=2)
    scale = jnp.exp(-temper * mine) / ANCHORS
    columns, path_wide, info, anc, dem, scale = lax.optimization_barrier((columns, path_wide, info, anc, dem, scale))
    (cost,) = kernel_call(
        functools.partial(spread_kernel, used), [((used, cols, 128), VM)], [], 4 << 20, [VM], (columns,)
    )
    diag = ((2 * STEPS, 2, cols, 128), VM)
    padded = cols + 2 * PAD
    pieces = ((cols // CH, 4 * rows, CH), VM)
    whole = (warm.shape, HB)
    g, d, lab, sums, labels = kernel_call(
        first_kernel,
        [diag, diag, ((2, cols, lanes), VM), pieces, whole],
        [(rows + 2 * FIRST, 2, padded, 128)],
        9 << 20, [SM] + [HB] * 5 + [VM] * 3, (info, own, *near, anc, dem, cost),
        sems=(rows + 2 * FIRST, 2),
    )
    g, d, lab, sums, labels = kernel_call(
        functools.partial(next_kernel, FIRST + 1, False),
        [diag, diag, ((2, cols, lanes), VM), pieces, whole],
        [(STEPS, 2, padded, 128), (1, 2, padded, 128)],
        5 << 20, [SM] + [VM] * 9 + [HB], (info, *later[0], anc, dem, cost, g, d, lab, sums, labels),
        {6: 0, 7: 1, 10: 4},
    )
    far, lab, sums, labels = kernel_call(
        functools.partial(next_kernel, FIRST + 2, True),
        [((2, 2, cols, 128), VM), ((2, cols, lanes), VM), pieces, whole],
        [(STEPS, 2, padded, 128), (1, 2, padded, 128)],
        5 << 20, [SM] + [VM] * 9 + [HB], (info, *later[1], anc, dem, cost, g, d, lab, sums, labels), {10: 3},
    )
    (sums,) = kernel_call(
        functools.partial(cross_kernel, FIRST + 3),
        [pieces], [], 2 << 20, [SM] + [VM] * 8,
        (info, *later[2], anc, dem, path_wide, far, lab, sums),
    )
    total = lax.all_to_all(sums, "org", split_axis=0, concat_axis=0, tiled=True).sum(axis=0)
    return labels, total.reshape(4, rows, width) * scale


def solution(mesh):
    placed = (P("blk", None, "org"), P(None, "blk", None), P("org"), P("org"))
    return jax.shard_map(
        local,
        mesh=mesh,
        in_specs=placed,
        out_specs=(P("blk", None, "org"), P(None, "blk", "org")),
        check_vma=False,
    )
```

```python
import functools
import jax
import jax.numpy as jnp
from jax import lax
from jax.experimental import pallas as pl
from jax.experimental.pallas import tpu as pltpu
from jax.sharding import PartitionSpec as P


ANCHORS = 1024
STEPS = 6
EDGE = 6
FIRST = 3
SECOND = STEPS - 1 - FIRST
PAD = 8
CH = 128
far_value = 1000000000.0
temper = 0.5
F32 = jnp.float32
WEST, EAST, NORTH, SOUTH = range(4)
OUTER = (NORTH, SOUTH)
INNER_SIDE = (SOUTH, NORTH)


def row_of(side, depth):
    return depth if side == 0 else 7 - depth


def cost_row(side, depth):
    return EDGE + row_of(side, depth)


def chunks(cols, body):
    def step(i, carry):
        body(pl.multiple_of(i * CH, CH))
        return carry

    lax.fori_loop(0, cols // CH, step, 0)


def half_lanes(h):
    return pl.ds(h * 128, 128)


def clear_pads(buf, rows, cols):
    zero = jnp.zeros((PAD, 128), F32)
    for r in range(rows):
        for h in range(2):
            buf[r, h, pl.ds(0, PAD), :] = zero
            buf[r, h, pl.ds(cols + PAD, PAD), :] = zero


def anchored(values, anchors, node0):
    ids = node0 + lax.broadcasted_iota(jnp.int32, values.shape, 0)
    return jnp.where(ids == anchors, 0.0, values)


def add_lane_sum(sums, side, row, piece, terms):
    at = side * 8 + row
    sums[piece, at : at + 1, :] += jnp.sum(terms, axis=1)[None, :]


def spread_kernel(picks, table, out_ref, sem):
    rest = jnp.zeros((128 - table.shape[0], CH), F32)

    def body(c0):
        block = jnp.concatenate([table[:, pl.ds(c0, CH)], rest]).T
        for n, lane in enumerate(picks):
            out_ref[n, pl.ds(c0, CH), :] = jnp.broadcast_to(block[:, lane : lane + 1], (CH, 128))

    chunks(table.shape[1], body)


def first_kernel(info, own, lead1, lead2, more1, more2, anchors, demand, cost, g_out, d_out, lab_out, sums, labels, buf, sem):
    cols = own.shape[1]
    rows = 8 + 2 * FIRST
    odd = info[1]
    north_of = (odd, 1 - odd)
    loads = []
    for i in range(8):
        loads.append((own, i, FIRST + i))
    for lead, more, north in ((lead1, more1, north_of[0]), (lead2, more2, north_of[1])):
        loads.append((lead, None, FIRST + 8 - north * 9))
        for i in range(FIRST - 1):
            loads.append((more, i, (FIRST + 9) * (1 - north) + i))
    loads = [
        pltpu.make_async_copy(
            ref.at[pl.ds(0, cols), half_lanes(h)] if i is None else ref.at[i, :, half_lanes(h)],
            buf.at[at, h, pl.ds(PAD, cols), :],
            sem.at[n, h],
        )
        for n, (ref, i, at) in enumerate(loads)
        for h in range(2)
    ]
    for copy in loads:
        copy.start()
    sums[...] = jnp.zeros(sums.shape, F32)
    clear_pads(buf, rows, cols)
    for copy in loads:
        copy.wait()

    def mark(i, carry):
        node0 = (info[0] + i - FIRST) * cols

        def body(c0):
            here = pl.ds(c0 + PAD, CH)
            for h in range(2):
                buf[i, h, here, :] = anchored(buf[i, h, here, :], anchors[:, half_lanes(h)], node0 + c0)

        chunks(cols, body)
        return carry

    lax.fori_loop(0, rows, mark, 0)
    for t in range(1, STEPS + 1):
        have = rows - 2 * (t - 1)
        for side in range(2):
            at, inner = (0, 1) if side == 0 else (have - 1, have - 2)
            j = 4 * (row_of(side, t - FIRST - 1) + EDGE)

            def edge(c0, side=side, at=at, inner=inner, j=j, t=t):
                here, mid = pl.ds(c0, CH), pl.ds(c0 + PAD, CH)
                west, east, within = (cost[j + k, here, :] for k in (WEST, EAST, INNER_SIDE[side]))
                for h in range(2):
                    centre = buf[at, h, mid, :]
                    g_out[side * STEPS + t - 1, h, here, :] = jnp.minimum(
                        jnp.minimum(centre, buf[at, h, pl.ds(c0 + PAD - 1, CH), :] + west),
                        jnp.minimum(buf[at, h, pl.ds(c0 + PAD + 1, CH), :] + east, buf[inner, h, mid, :] + within),
                    )
                    d_out[side * STEPS + t - 1, h, here, :] = centre

            chunks(cols, edge)

        def row(i, carry, t=t):
            j = 4 * (i + t - FIRST + EDGE)

            def body(c0):
                here, mid = pl.ds(c0, CH), pl.ds(c0 + PAD, CH)
                west, east, up, down = (cost[j + k, here, :] for k in (WEST, EAST, NORTH, SOUTH))
                for h in range(2):
                    buf[i, h, mid, :] = jnp.minimum(
                        jnp.minimum(
                            jnp.minimum(buf[i + 1, h, mid, :], buf[i + 1, h, pl.ds(c0 + PAD - 1, CH), :] + west),
                            jnp.minimum(buf[i + 1, h, pl.ds(c0 + PAD + 1, CH), :] + east, buf[i, h, mid, :] + up),
                        ),
                        buf[i + 2, h, mid, :] + down,
                    )

            chunks(cols, body)
            return carry

        lax.fori_loop(0, have - 2, row, 0)

    done = 2 * FIRST - 4
    first_done = STEPS - FIRST
    stores = [
        pltpu.make_async_copy(
            buf.at[r, h, pl.ds(PAD, cols), :], labels.at[r + first_done, :, half_lanes(h)], sem.at[r, h]
        )
        for r in range(done)
        for h in range(2)
    ]
    for copy in stores:
        copy.start()

    def final(c0):
        for r in range(done):
            for h in range(2):
                value = buf[r, h, pl.ds(c0 + PAD, CH), :]
                for n, kept in enumerate((0, done - 1)):
                    if r == kept:
                        lab_out[n, pl.ds(c0, CH), half_lanes(h)] = value
                buf[r + done, h, pl.ds(c0 + PAD, CH), :] = jnp.exp(-temper * value)

    chunks(cols, final)

    def link(c0):
        piece = c0 // CH
        mid = pl.ds(c0 + PAD, CH)
        for r in range(done):
            inv = [demand[:, half_lanes(h)] * jnp.exp(temper * buf[r, h, mid, :]) for h in range(2)]

            def add(side, shift, other, inv=inv, r=r):
                terms = [inv[h] * buf[other + done, h, pl.ds(c0 + PAD + shift, CH), :] for h in range(2)]
                add_lane_sum(sums, side, r + first_done, piece, terms[0] + terms[1])

            add(WEST, -1, r)
            add(EAST, 1, r)
            if r > 0:
                add(NORTH, 0, r - 1)
            if r < done - 1:
                add(SOUTH, 0, r + 1)

    chunks(cols, link)
    for copy in stores:
        copy.wait()


def pick(got1, got2, odd, side, place, here, lanes):
    at = got1.shape[0] - 1 - place if side == 0 else place
    one, two = got1[at, here, lanes], got2[at, here, lanes]
    return jnp.where(odd, one, two) if side == 0 else jnp.where(odd, two, one)


def next_kernel(depth, place, last, *refs):
    info, got1, got2, anchors, demand, cost, g_in, d_in, in_lab, sums_in, _ = refs[:11]
    if last:
        far_out, lab_out, sums, labels, dbuf, ebuf, sem = refs[11:]
    else:
        g_out, d_out, lab_out, sums, labels, dbuf, ebuf, sem = refs[11:]
    cols = got1.shape[1]
    odd = info[1] > 0
    at_rows = tuple(row_of(side, STEPS - depth) for side in range(2))
    sums[...] = sums_in[...]
    stores = [pltpu.make_async_copy(lab_out.at[n], labels.at[at_rows[n]], sem.at[n]) for n in range(2)]
    clear_pads(dbuf, STEPS, cols)
    clear_pads(ebuf, 1, cols)
    for side in range(2):
        within = 0 if side == 0 else in_lab.shape[0] - 1
        node0 = (info[0] + row_of(side, -depth)) * cols

        def chain(c0, side=side, node0=node0):
            here, mid = pl.ds(c0, CH), pl.ds(c0 + PAD, CH)
            values = []
            for h in range(2):
                values.append(anchored(pick(got1, got2, odd, side, place, here, half_lanes(h)), anchors[:, half_lanes(h)], node0 + c0))
                dbuf[0, h, mid, :] = values[h]
            for t in range(1, STEPS + 1):
                outer = cost[4 * cost_row(side, t - depth) + OUTER[side], here, :]
                for h in range(2):
                    values[h] = jnp.minimum(g_in[side * STEPS + t - 1, h, here, :], values[h] + outer)
                    if t < STEPS:
                        dbuf[t, h, mid, :] = values[h]
            for h in range(2):
                lab_out[side, here, half_lanes(h)] = values[h]
                ebuf[0, h, mid, :] = jnp.exp(-temper * values[h])

        chunks(cols, chain)
        stores[side].start()

        def ahead(c0, side=side):
            here, mid = pl.ds(c0, CH), pl.ds(c0 + PAD, CH)
            best = [None, None]
            for t in range(1, STEPS + 1):
                j = 4 * cost_row(side, t - depth - 1)
                west, east, inner = (cost[j + k, here, :] for k in (WEST, EAST, INNER_SIDE[side]))
                outer = cost[j + OUTER[side], here, :] if last and t > 1 else None
                for h in range(2):
                    centre = dbuf[t - 1, h, mid, :]
                    found = jnp.minimum(
                        jnp.minimum(centre, dbuf[t - 1, h, pl.ds(c0 + PAD - 1, CH), :] + west),
                        jnp.minimum(
                            dbuf[t - 1, h, pl.ds(c0 + PAD + 1, CH), :] + east,
                            d_in[side * STEPS + t - 1, h, here, :] + inner,
                        ),
                    )
                    if not last:
                        g_out[side * STEPS + t - 1, h, here, :] = found
                        d_out[side * STEPS + t - 1, h, here, :] = centre
                    else:
                        best[h] = found if t == 1 else jnp.minimum(found, best[h] + outer)
            if last:
                for h in range(2):
                    far_out[side, h, here, :] = best[h]

        chunks(cols, ahead)

        def link(c0, side=side, within=within):
            here, mid = pl.ds(c0, CH), pl.ds(c0 + PAD, CH)
            piece = c0 // CH
            at = at_rows[side]
            inside = row_of(side, STEPS - depth + 1)
            terms = [0.0] * 4
            for h in range(2):
                dem = demand[:, half_lanes(h)]
                inv = dem * jnp.exp(temper * lab_out[side, here, half_lanes(h)])
                other = in_lab[within, here, half_lanes(h)]
                terms[0] += inv * ebuf[0, h, pl.ds(c0 + PAD - 1, CH), :]
                terms[1] += inv * ebuf[0, h, pl.ds(c0 + PAD + 1, CH), :]
                terms[2] += inv * jnp.exp(-temper * other)
                terms[3] += dem * jnp.exp(temper * other) * ebuf[0, h, mid, :]
            add_lane_sum(sums, WEST, at, piece, terms[0])
            add_lane_sum(sums, EAST, at, piece, terms[1])
            add_lane_sum(sums, INNER_SIDE[side], at, piece, terms[2])
            add_lane_sum(sums, OUTER[side], inside, piece, terms[3])

        chunks(cols, link)

    for copy in stores:
        copy.wait()


def cross_kernel(depth, info, got1, got2, anchors, demand, path, far_in, lab, sums_in, sums, sem):
    cols = got1.shape[1]
    odd = info[1] > 0
    sums[...] = sums_in[...]

    def body(c0):
        here = pl.ds(c0, CH)
        for side in range(2):
            node0 = (info[0] + row_of(side, -depth)) * cols
            terms = 0.0
            for h in range(2):
                lanes = half_lanes(h)
                value = pick(got1, got2, odd, side, 0, here, lanes)
                value = anchored(value, anchors[:, lanes], node0 + c0) + path[side, here, :]
                value = jnp.minimum(value, far_in[side, h, here, :])
                terms += demand[:, lanes] * jnp.exp(temper * lab[side, here, lanes]) * jnp.exp(-temper * value)
            add_lane_sum(sums, OUTER[side], row_of(side, 0), c0 // CH, terms)

    chunks(cols, body)


VM = pl.BlockSpec(memory_space=pltpu.VMEM)
SM = pl.BlockSpec(memory_space=pltpu.SMEM)
HB = pl.BlockSpec(memory_space=pltpu.HBM)


def kernel_call(body, outs, scratch, limit, specs, args, aliases=None, sems=(4,)):
    return pl.pallas_call(
        body,
        out_shape=[
            jax.ShapeDtypeStruct(shape, F32) if spec is HB else pltpu.VMEM(shape, F32) for shape, spec in outs
        ],
        in_specs=specs,
        out_specs=[spec for _, spec in outs],
        scratch_shapes=[pltpu.VMEM(s, F32) for s in scratch] + [pltpu.SemaphoreType.DMA(sems)],
        compiler_params=pltpu.CompilerParams(vmem_limit_bytes=limit),
        cost_estimate=pl.CostEstimate(flops=1 << 20, bytes_accessed=32 << 20, transcendentals=0),
        input_output_aliases=aliases or {},
    )(*(pltpu.with_memory_space_constraint(v, pltpu.HBM) if spec is HB else v for v, spec in zip(args, specs)))


def local(warm, link_costs, anchor_nodes, demand):
    rows, cols, lanes = warm.shape
    count = lax.axis_size("blk")
    me = lax.axis_index("blk")
    swaps = [[(i + a, i + 1 - a) for i in range(first, count - 1, 2) for a in (0, 1)] for first in (0, 1)]
    odd = me % 2
    own = warm

    def swap(number, message):
        return lax.ppermute(message, "blk", swaps[number])

    def cut(array, number, first, size, axis):
        low, high = first - 1, rows - first - size + 1
        start = jnp.where(odd == number, high, low)
        return lax.dynamic_slice_in_dim(array, start, size, axis)

    def lead_of(number):
        parts = [flat_costs[:, n : n + lanes] for n in range(0, cols, lanes)]
        return jnp.concatenate([cut(warm, number, 1, 1, 0)[0], *parts])

    flat_costs = link_costs.reshape(4 * rows, cols)
    lead = [lead_of(number) for number in range(2)]
    got_lead = [swap(number, lead[number]) for number in range(2)]
    warm, lead = lax.optimization_barrier((warm, lead))

    def exchange(first, size):
        return [swap(number, cut(warm, number, first, size, 0)) for number in range(2)]

    near = [*got_lead, *exchange(2, FIRST - 1)]
    later = {k: exchange(k, SECOND if k == FIRST + 1 else 1) for k in (FIRST + 1, STEPS, STEPS + 1)}
    got_costs = [
        jnp.concatenate([m[n : n + 4 * rows] for n in range(cols, m.shape[0], 4 * rows)], axis=1) for m in got_lead
    ]
    cost_n = jnp.where(odd == 1, got_costs[0], got_costs[1]).reshape(4, rows, cols)
    cost_s = jnp.where(odd == 1, got_costs[1], got_costs[0]).reshape(4, rows, cols)

    row = (me * rows + jnp.arange(rows))[:, None]
    col = jnp.arange(cols)[None, :]
    wide = (rows, cols)
    wall = jnp.stack(
        [
            jnp.broadcast_to(col == 0, wide),
            jnp.broadcast_to(col == cols - 1, wide),
            jnp.broadcast_to(row == 0, wide),
            jnp.broadcast_to(row == rows * count - 1, wide),
        ]
    )
    own_costs = jnp.where(wall, far_value, link_costs)
    sides = ((col == 0)[None], (col == cols - 1)[None])
    cost_n, cost_s = (
        jnp.concatenate([*(jnp.where(w, far_value, c[k : k + 1]) for k, w in enumerate(sides)), c[2:]]) for c in (cost_n, cost_s)
    )
    path = jnp.stack([cost_n[NORTH, rows - EDGE :].sum(axis=0), cost_s[SOUTH, :EDGE].sum(axis=0)])
    table = jnp.concatenate([cost_n, own_costs, cost_s], axis=1).reshape(-1, cols)
    total = 3 * rows
    used = [k * total + r for r in range(rows - EDGE, 2 * rows + EDGE) for k in range(4)]
    path_wide = jnp.broadcast_to(path[:, :, None], (2, cols, 128))
    info = jnp.stack([me * rows, odd]).astype(jnp.int32)
    anc = anchor_nodes.reshape(1, lanes)
    dem = demand.reshape(1, lanes)
    owners = lax.axis_size("org")
    width = cols // owners
    mine = lax.dynamic_slice_in_dim(own_costs, lax.axis_index("org") * width, width, axis=2)
    scale = jnp.exp(-temper * mine) / ANCHORS
    table, path_wide, info, anc, dem, scale = lax.optimization_barrier((table, path_wide, info, anc, dem, scale))
    (cost,) = kernel_call(
        functools.partial(spread_kernel, used), [((len(used), cols, 128), VM)], [], 1 << 20, [VM], (table,)
    )
    diag = ((2 * STEPS, 2, cols, 128), VM)
    padded = cols + 2 * PAD
    pieces = ((cols // CH, 4 * rows, CH), VM)
    whole = (warm.shape, HB)
    g, d, lab, sums, labels = kernel_call(
        first_kernel,
        [diag, diag, ((2, cols, lanes), VM), pieces, whole],
        [(rows + 2 * FIRST, 2, padded, 128)],
        7680 << 10, [SM] + [HB] * 5 + [VM] * 3, (info, own, *near, anc, dem, cost),
        sems=(rows + 2 * FIRST, 2),
    )
    for place in range(SECOND):
        depth = FIRST + 1 + place
        g, d, lab, sums, labels = kernel_call(
            functools.partial(next_kernel, depth, place, False),
            [diag, diag, ((2, cols, lanes), VM), pieces, whole],
            [(STEPS, 2, padded, 128), (1, 2, padded, 128)],
            5 << 20, [SM] + [VM] * 9 + [HB],
            (info, *later[FIRST + 1], anc, dem, cost, g, d, lab, sums, labels),
            {6: 0, 7: 1, 10: 4},
        )
    far, lab, sums, labels = kernel_call(
        functools.partial(next_kernel, STEPS, 0, True),
        [((2, 2, cols, 128), VM), ((2, cols, lanes), VM), pieces, whole],
        [(STEPS, 2, padded, 128), (1, 2, padded, 128)],
        5 << 20, [SM] + [VM] * 9 + [HB], (info, *later[STEPS], anc, dem, cost, g, d, lab, sums, labels), {10: 3},
    )
    (sums,) = kernel_call(
        functools.partial(cross_kernel, STEPS + 1),
        [pieces], [], 2 << 20, [SM] + [VM] * 8,
        (info, *later[STEPS + 1], anc, dem, path_wide, far, lab, sums),
    )
    total = lax.all_to_all(sums, "org", split_axis=0, concat_axis=0, tiled=True).sum(axis=0)
    return labels, total.reshape(4, rows, width) * scale


def solution(mesh):
    placed = (P("blk", None, "org"), P(None, "blk", None), P("org"), P("org"))
    return jax.shard_map(
        local,
        mesh=mesh,
        in_specs=placed,
        out_specs=(P("blk", None, "org"), P(None, "blk", "org")),
        check_vma=False,
    )
```

```python
import functools
import jax
import jax.numpy as jnp
from jax import lax
from jax.experimental import pallas as pl
from jax.experimental.pallas import tpu as pltpu
from jax.sharding import PartitionSpec as P


ANCHORS = 1024
STEPS = 6
EDGE = 6
FIRST = 3
SECOND = STEPS - 1 - FIRST
PAD = 8
CH = 128
far_value = 1000000000.0
temper = 0.5
F32 = jnp.float32
WEST, EAST, NORTH, SOUTH = range(4)
OUTER = (NORTH, SOUTH)
INNER_SIDE = (SOUTH, NORTH)


def row_of(side, depth):
    return depth if side == 0 else 7 - depth


def cost_row(side, depth):
    return EDGE + row_of(side, depth)


def chunks(cols, body):
    def step(i, carry):
        body(pl.multiple_of(i * CH, CH))
        return carry

    lax.fori_loop(0, cols // CH, step, 0)


def half_lanes(h):
    return pl.ds(h * 128, 128)


def clear_pads(buf, rows, cols):
    zero = jnp.zeros((PAD, 128), F32)
    for r in range(rows):
        for h in range(2):
            buf[r, h, pl.ds(0, PAD), :] = zero
            buf[r, h, pl.ds(cols + PAD, PAD), :] = zero


def anchored(values, anchors, node0):
    ids = node0 + lax.broadcasted_iota(jnp.int32, values.shape, 0)
    return jnp.where(ids == anchors, 0.0, values)


def add_lane_sum(sums, side, row, piece, terms):
    at = side * 8 + row
    sums[piece, at : at + 1, :] += jnp.sum(terms, axis=1)[None, :]


def lead_kernel(info, own, costs, lead1, lead2, sem):
    rows, cols, lanes = own.shape
    copies = []
    for number, out in ((1, lead2), (0, lead1)):
        start = jnp.where(info[1] == number, rows - 1, 0)
        copies.append(pltpu.make_async_copy(own.at[start], out.at[pl.ds(0, cols), :], sem.at[number, 0]))
        for n in range(cols // lanes):
            place = pl.ds(cols + n * costs.shape[0], costs.shape[0])
            copies.append(
                pltpu.make_async_copy(costs.at[:, pl.ds(n * lanes, lanes)], out.at[place, :], sem.at[number, n + 1])
            )
    for copy in copies:
        copy.start()
    for copy in copies:
        copy.wait()


def spread_kernel(picks, table, out_ref, sem):
    rest = jnp.zeros((128 - table.shape[0], CH), F32)

    def body(c0):
        block = jnp.concatenate([table[:, pl.ds(c0, CH)], rest]).T
        for n, lane in enumerate(picks):
            out_ref[n, pl.ds(c0, CH), :] = jnp.broadcast_to(block[:, lane : lane + 1], (CH, 128))

    chunks(table.shape[1], body)


def first_kernel(info, own, lead1, lead2, more1, more2, anchors, demand, cost, g_out, d_out, lab_out, sums, labels, buf, sem):
    cols = own.shape[1]
    rows = 8 + 2 * FIRST
    odd = info[1]
    north_of = (odd, 1 - odd)
    loads = []
    for i in range(8):
        loads.append((own, i, FIRST + i))
    for lead, more, north in ((lead1, more1, north_of[0]), (lead2, more2, north_of[1])):
        loads.append((lead, None, FIRST + 8 - north * 9))
        for i in range(FIRST - 1):
            loads.append((more, i, (FIRST + 9) * (1 - north) + i))
    loads = [
        pltpu.make_async_copy(
            ref.at[pl.ds(0, cols), half_lanes(h)] if i is None else ref.at[i, :, half_lanes(h)],
            buf.at[at, h, pl.ds(PAD, cols), :],
            sem.at[n, h],
        )
        for n, (ref, i, at) in enumerate(loads)
        for h in range(2)
    ]
    for copy in loads:
        copy.start()
    sums[...] = jnp.zeros(sums.shape, F32)
    clear_pads(buf, rows, cols)
    for copy in loads:
        copy.wait()

    def mark(i, carry):
        node0 = (info[0] + i - FIRST) * cols

        def body(c0):
            here = pl.ds(c0 + PAD, CH)
            for h in range(2):
                buf[i, h, here, :] = anchored(buf[i, h, here, :], anchors[:, half_lanes(h)], node0 + c0)

        chunks(cols, body)
        return carry

    lax.fori_loop(0, rows, mark, 0)
    for t in range(1, STEPS + 1):
        have = rows - 2 * (t - 1)
        for side in range(2):
            at, inner = (0, 1) if side == 0 else (have - 1, have - 2)
            j = 4 * (row_of(side, t - FIRST - 1) + EDGE)

            def edge(c0, side=side, at=at, inner=inner, j=j, t=t):
                here, mid = pl.ds(c0, CH), pl.ds(c0 + PAD, CH)
                west, east, within = (cost[j + k, here, :] for k in (WEST, EAST, INNER_SIDE[side]))
                for h in range(2):
                    centre = buf[at, h, mid, :]
                    g_out[side * STEPS + t - 1, h, here, :] = jnp.minimum(
                        jnp.minimum(centre, buf[at, h, pl.ds(c0 + PAD - 1, CH), :] + west),
                        jnp.minimum(buf[at, h, pl.ds(c0 + PAD + 1, CH), :] + east, buf[inner, h, mid, :] + within),
                    )
                    d_out[side * STEPS + t - 1, h, here, :] = centre

            chunks(cols, edge)

        def row(i, carry, t=t):
            j = 4 * (i + t - FIRST + EDGE)

            def body(c0):
                here, mid = pl.ds(c0, CH), pl.ds(c0 + PAD, CH)
                west, east, up, down = (cost[j + k, here, :] for k in (WEST, EAST, NORTH, SOUTH))
                for h in range(2):
                    buf[i, h, mid, :] = jnp.minimum(
                        jnp.minimum(
                            jnp.minimum(buf[i + 1, h, mid, :], buf[i + 1, h, pl.ds(c0 + PAD - 1, CH), :] + west),
                            jnp.minimum(buf[i + 1, h, pl.ds(c0 + PAD + 1, CH), :] + east, buf[i, h, mid, :] + up),
                        ),
                        buf[i + 2, h, mid, :] + down,
                    )

            chunks(cols, body)
            return carry

        lax.fori_loop(0, have - 2, row, 0)

    done = 2 * FIRST - 4
    first_done = STEPS - FIRST
    stores = [
        pltpu.make_async_copy(
            buf.at[r, h, pl.ds(PAD, cols), :], labels.at[r + first_done, :, half_lanes(h)], sem.at[r, h]
        )
        for r in range(done)
        for h in range(2)
    ]
    for copy in stores:
        copy.start()

    def final(c0):
        for r in range(done):
            for h in range(2):
                value = buf[r, h, pl.ds(c0 + PAD, CH), :]
                for n, kept in enumerate((0, done - 1)):
                    if r == kept:
                        lab_out[n, pl.ds(c0, CH), half_lanes(h)] = value
                buf[r + done, h, pl.ds(c0 + PAD, CH), :] = jnp.exp(-temper * value)

    chunks(cols, final)

    def link(c0):
        piece = c0 // CH
        mid = pl.ds(c0 + PAD, CH)
        for r in range(done):
            inv = [demand[:, half_lanes(h)] * jnp.exp(temper * buf[r, h, mid, :]) for h in range(2)]

            def add(side, shift, other, inv=inv, r=r):
                terms = [inv[h] * buf[other + done, h, pl.ds(c0 + PAD + shift, CH), :] for h in range(2)]
                add_lane_sum(sums, side, r + first_done, piece, terms[0] + terms[1])

            add(WEST, -1, r)
            add(EAST, 1, r)
            if r > 0:
                add(NORTH, 0, r - 1)
            if r < done - 1:
                add(SOUTH, 0, r + 1)

    chunks(cols, link)
    for copy in stores:
        copy.wait()


def pick(got1, got2, odd, side, place, here, lanes):
    at = got1.shape[0] - 1 - place if side == 0 else place
    one, two = got1[at, here, lanes], got2[at, here, lanes]
    return jnp.where(odd, one, two) if side == 0 else jnp.where(odd, two, one)


def next_kernel(depth, place, last, *refs):
    info, got1, got2, anchors, demand, cost, g_in, d_in, in_lab, sums_in, _ = refs[:11]
    if last:
        far_out, lab_out, sums, labels, dbuf, ebuf, sem = refs[11:]
    else:
        g_out, d_out, lab_out, sums, labels, dbuf, ebuf, sem = refs[11:]
    cols = got1.shape[1]
    odd = info[1] > 0
    at_rows = tuple(row_of(side, STEPS - depth) for side in range(2))
    sums[...] = sums_in[...]
    stores = [pltpu.make_async_copy(lab_out.at[n], labels.at[at_rows[n]], sem.at[n]) for n in range(2)]
    clear_pads(dbuf, STEPS, cols)
    clear_pads(ebuf, 1, cols)
    for side in range(2):
        within = 0 if side == 0 else in_lab.shape[0] - 1
        node0 = (info[0] + row_of(side, -depth)) * cols

        def chain(c0, side=side, node0=node0):
            here, mid = pl.ds(c0, CH), pl.ds(c0 + PAD, CH)
            values = []
            for h in range(2):
                values.append(anchored(pick(got1, got2, odd, side, place, here, half_lanes(h)), anchors[:, half_lanes(h)], node0 + c0))
                dbuf[0, h, mid, :] = values[h]
            for t in range(1, STEPS + 1):
                outer = cost[4 * cost_row(side, t - depth) + OUTER[side], here, :]
                for h in range(2):
                    values[h] = jnp.minimum(g_in[side * STEPS + t - 1, h, here, :], values[h] + outer)
                    if t < STEPS:
                        dbuf[t, h, mid, :] = values[h]
            for h in range(2):
                lab_out[side, here, half_lanes(h)] = values[h]
                ebuf[0, h, mid, :] = jnp.exp(-temper * values[h])

        chunks(cols, chain)
        stores[side].start()

        def ahead(c0, side=side):
            here, mid = pl.ds(c0, CH), pl.ds(c0 + PAD, CH)
            best = [None, None]
            for t in range(1, STEPS + 1):
                j = 4 * cost_row(side, t - depth - 1)
                west, east, inner = (cost[j + k, here, :] for k in (WEST, EAST, INNER_SIDE[side]))
                outer = cost[j + OUTER[side], here, :] if last and t > 1 else None
                for h in range(2):
                    centre = dbuf[t - 1, h, mid, :]
                    found = jnp.minimum(
                        jnp.minimum(centre, dbuf[t - 1, h, pl.ds(c0 + PAD - 1, CH), :] + west),
                        jnp.minimum(
                            dbuf[t - 1, h, pl.ds(c0 + PAD + 1, CH), :] + east,
                            d_in[side * STEPS + t - 1, h, here, :] + inner,
                        ),
                    )
                    if not last:
                        g_out[side * STEPS + t - 1, h, here, :] = found
                        d_out[side * STEPS + t - 1, h, here, :] = centre
                    else:
                        best[h] = found if t == 1 else jnp.minimum(found, best[h] + outer)
            if last:
                for h in range(2):
                    far_out[side, h, here, :] = best[h]

        chunks(cols, ahead)

        def link(c0, side=side, within=within):
            here, mid = pl.ds(c0, CH), pl.ds(c0 + PAD, CH)
            piece = c0 // CH
            at = at_rows[side]
            inside = row_of(side, STEPS - depth + 1)
            terms = [0.0] * 4
            for h in range(2):
                dem = demand[:, half_lanes(h)]
                inv = dem * jnp.exp(temper * lab_out[side, here, half_lanes(h)])
                other = in_lab[within, here, half_lanes(h)]
                terms[0] += inv * ebuf[0, h, pl.ds(c0 + PAD - 1, CH), :]
                terms[1] += inv * ebuf[0, h, pl.ds(c0 + PAD + 1, CH), :]
                terms[2] += inv * jnp.exp(-temper * other)
                terms[3] += dem * jnp.exp(temper * other) * ebuf[0, h, mid, :]
            add_lane_sum(sums, WEST, at, piece, terms[0])
            add_lane_sum(sums, EAST, at, piece, terms[1])
            add_lane_sum(sums, INNER_SIDE[side], at, piece, terms[2])
            add_lane_sum(sums, OUTER[side], inside, piece, terms[3])

        chunks(cols, link)

    for copy in stores:
        copy.wait()


def cross_kernel(depth, info, got1, got2, anchors, demand, cost, far_in, lab, sums_in, sums, sem):
    cols = got1.shape[1]
    odd = info[1] > 0
    sums[...] = sums_in[...]

    def body(c0):
        here = pl.ds(c0, CH)
        for side in range(2):
            node0 = (info[0] + row_of(side, -depth)) * cols
            terms = 0.0
            for h in range(2):
                lanes = half_lanes(h)
                value = pick(got1, got2, odd, side, 0, here, lanes)
                value = anchored(value, anchors[:, lanes], node0 + c0) + cost[4 * cost_row(side, -EDGE) + OUTER[side], here, :]
                value = jnp.minimum(value, far_in[side, h, here, :])
                terms += demand[:, lanes] * jnp.exp(temper * (lab[side, here, lanes] - value))
            add_lane_sum(sums, OUTER[side], row_of(side, 0), c0 // CH, terms)

    chunks(cols, body)


VM = pl.BlockSpec(memory_space=pltpu.VMEM)
SM = pl.BlockSpec(memory_space=pltpu.SMEM)
HB = pl.BlockSpec(memory_space=pltpu.HBM)


def kernel_call(body, outs, scratch, limit, specs, args, aliases=None, sems=(4,)):
    return pl.pallas_call(
        body,
        out_shape=[
            jax.ShapeDtypeStruct(shape, F32) if spec is HB else pltpu.VMEM(shape, F32) for shape, spec in outs
        ],
        in_specs=specs,
        out_specs=[spec for _, spec in outs],
        scratch_shapes=[pltpu.VMEM(s, F32) for s in scratch] + [pltpu.SemaphoreType.DMA(sems)],
        compiler_params=pltpu.CompilerParams(vmem_limit_bytes=limit),
        cost_estimate=pl.CostEstimate(flops=1 << 20, bytes_accessed=32 << 20, transcendentals=0),
        input_output_aliases=aliases or {},
    )(*(pltpu.with_memory_space_constraint(v, pltpu.HBM) if spec is HB else v for v, spec in zip(args, specs)))


def local(warm, link_costs, anchor_nodes, demand):
    rows, cols, lanes = warm.shape
    count = lax.axis_size("blk")
    me = lax.axis_index("blk")
    swaps = [[(i + a, i + 1 - a) for i in range(first, count - 1, 2) for a in (0, 1)] for first in (0, 1)]
    odd = me % 2
    own = warm

    def swap(number, message):
        return lax.ppermute(message, "blk", swaps[number])

    def cut(array, number, first, size, axis):
        low, high = first - 1, rows - first - size + 1
        start = jnp.where(odd == number, high, low)
        return lax.dynamic_slice_in_dim(array, start, size, axis)

    info = jnp.stack([me * rows, odd]).astype(jnp.int32)
    flat_costs = link_costs.reshape(4 * rows, cols)
    message = ((cols + 4 * rows * cols // lanes, lanes), VM)
    lead = kernel_call(
        lead_kernel, [message] * 2, [], 1 << 20, [SM, HB, HB], (info, warm, flat_costs), sems=(2, 1 + cols // lanes)
    )
    got_lead = [swap(number, lead[number]) for number in range(2)]
    warm, lead = lax.optimization_barrier((warm, lead))

    def exchange(first, size):
        return [swap(number, cut(warm, number, first, size, 0)) for number in range(2)]

    near = [*got_lead, *exchange(2, FIRST - 1)]
    later = {k: exchange(k, SECOND if k == FIRST + 1 else 1) for k in (FIRST + 1, STEPS, STEPS + 1)}
    got_costs = [
        jnp.concatenate([m[n : n + 4 * rows] for n in range(cols, m.shape[0], 4 * rows)], axis=1) for m in got_lead
    ]
    cost_n = jnp.where(odd == 1, got_costs[0], got_costs[1]).reshape(4, rows, cols)
    cost_s = jnp.where(odd == 1, got_costs[1], got_costs[0]).reshape(4, rows, cols)

    row = (me * rows + jnp.arange(rows))[:, None]
    col = jnp.arange(cols)[None, :]
    wide = (rows, cols)
    wall = jnp.stack(
        [
            jnp.broadcast_to(col == 0, wide),
            jnp.broadcast_to(col == cols - 1, wide),
            jnp.broadcast_to(row == 0, wide),
            jnp.broadcast_to(row == rows * count - 1, wide),
        ]
    )
    own_costs = jnp.where(wall, far_value, link_costs)
    sides = ((col == 0)[None], (col == cols - 1)[None])
    cost_n, cost_s = (
        jnp.concatenate([*(jnp.where(w, far_value, c[k : k + 1]) for k, w in enumerate(sides)), c[2:]]) for c in (cost_n, cost_s)
    )
    cost_n = cost_n.at[NORTH, rows - EDGE].set(cost_n[NORTH, rows - EDGE :].sum(axis=0))
    cost_s = cost_s.at[SOUTH, EDGE - 1].set(cost_s[SOUTH, :EDGE].sum(axis=0))
    table = jnp.concatenate([cost_n, own_costs, cost_s], axis=1).reshape(-1, cols)
    total = 3 * rows
    used = [k * total + r for r in range(rows - EDGE, 2 * rows + EDGE) for k in range(4)]
    anc = anchor_nodes.reshape(1, lanes)
    dem = demand.reshape(1, lanes)
    owners = lax.axis_size("org")
    width = cols // owners
    mine = lax.dynamic_slice_in_dim(own_costs, lax.axis_index("org") * width, width, axis=2)
    scale = jnp.exp(-temper * mine) / ANCHORS
    table, info, anc, dem, scale = lax.optimization_barrier((table, info, anc, dem, scale))
    (cost,) = kernel_call(
        functools.partial(spread_kernel, used), [((len(used), cols, 128), VM)], [], 1 << 20, [VM], (table,)
    )
    diag = ((2 * STEPS, 2, cols, 128), VM)
    padded = cols + 2 * PAD
    pieces = ((cols // CH, 4 * rows, CH), VM)
    whole = (warm.shape, HB)
    g, d, lab, sums, labels = kernel_call(
        first_kernel,
        [diag, diag, ((2, cols, lanes), VM), pieces, whole],
        [(rows + 2 * FIRST, 2, padded, 128)],
        7680 << 10, [SM] + [HB] * 5 + [VM] * 3, (info, own, *near, anc, dem, cost),
        sems=(rows + 2 * FIRST, 2),
    )
    for place in range(SECOND):
        depth = FIRST + 1 + place
        g, d, lab, sums, labels = kernel_call(
            functools.partial(next_kernel, depth, place, False),
            [diag, diag, ((2, cols, lanes), VM), pieces, whole],
            [(STEPS, 2, padded, 128), (1, 2, padded, 128)],
            5 << 20, [SM] + [VM] * 9 + [HB],
            (info, *later[FIRST + 1], anc, dem, cost, g, d, lab, sums, labels),
            {6: 0, 7: 1, 10: 4},
        )
    far, lab, sums, labels = kernel_call(
        functools.partial(next_kernel, STEPS, 0, True),
        [((2, 2, cols, 128), VM), ((2, cols, lanes), VM), pieces, whole],
        [(STEPS, 2, padded, 128), (1, 2, padded, 128)],
        5 << 20, [SM] + [VM] * 9 + [HB], (info, *later[STEPS], anc, dem, cost, g, d, lab, sums, labels), {10: 3},
    )
    (sums,) = kernel_call(
        functools.partial(cross_kernel, STEPS + 1), [pieces], [],
        2 << 20, [SM] + [VM] * 8, (info, *later[STEPS + 1], anc, dem, cost, far, lab, sums),
    )
    total, bit, at = sums, 1, lax.axis_index("org")
    while bit < owners:
        pairs = total.reshape(-1, 2, 4 * rows, CH)
        mine = at // bit % 2
        keep, send = (lax.dynamic_index_in_dim(pairs, n, 1, False) for n in (mine, 1 - mine))
        total = keep + lax.ppermute(send, "org", [(i, i ^ bit) for i in range(owners)])
        bit *= 2
    return labels, total.reshape(4, rows, width) * scale


def solution(mesh):
    placed = (P("blk", None, "org"), P(None, "blk", None), P("org"), P("org"))
    return jax.shard_map(
        local,
        mesh=mesh,
        in_specs=placed,
        out_specs=(P("blk", None, "org"), P(None, "blk", "org")),
        check_vma=False,
    )
```

```python
import functools
import jax
import jax.numpy as jnp
from jax import lax
from jax.experimental import pallas as pl
from jax.experimental.pallas import tpu as pltpu
from jax.sharding import PartitionSpec as P


ANCHORS = 1024
STEPS = 6
EDGE = 6
FIRST = 3
SECOND = STEPS - 1 - FIRST
PAD = 8
CH = 128
far_value = 1000000000.0
temper = 0.5
F32 = jnp.float32
WEST, EAST, NORTH, SOUTH = range(4)
OUTER = (NORTH, SOUTH)
INNER_SIDE = (SOUTH, NORTH)


def row_of(side, depth):
    return depth if side == 0 else 7 - depth


def cost_row(side, depth):
    return EDGE + row_of(side, depth)


def chunks(cols, body):
    def step(i, carry):
        body(pl.multiple_of(i * CH, CH))
        return carry

    lax.fori_loop(0, cols // CH, step, 0)


def half_lanes(h):
    return pl.ds(h * 128, 128)


def clear_pads(buf, rows, cols):
    zero = jnp.zeros((PAD, 128), F32)
    for r in range(rows):
        for h in range(2):
            buf[r, h, pl.ds(0, PAD), :] = zero
            buf[r, h, pl.ds(cols + PAD, PAD), :] = zero


def anchored(values, anchors, node0):
    ids = node0 + lax.broadcasted_iota(jnp.int32, values.shape, 0)
    return jnp.where(ids == anchors, 0.0, values)


def add_lane_sum(sums, side, row, piece, terms):
    at = side * 8 + row
    sums[piece, at : at + 1, :] += jnp.sum(terms, axis=1)[None, :]


def lead_kernel(info, own, costs, lead1, lead2, sem):
    rows, cols, lanes = own.shape
    copies = []
    for number, out in ((1, lead2), (0, lead1)):
        start = jnp.where(info[1] == number, rows - 1, 0)
        copies.append(pltpu.make_async_copy(own.at[start], out.at[pl.ds(0, cols), :], sem.at[number, 0]))
        for n in range(cols // lanes):
            place = pl.ds(cols + n * costs.shape[0], costs.shape[0])
            copies.append(
                pltpu.make_async_copy(costs.at[:, pl.ds(n * lanes, lanes)], out.at[place, :], sem.at[number, n + 1])
            )
    for copy in copies:
        copy.start()
    for copy in copies:
        copy.wait()


def spread_kernel(picks, table, out_ref, sem):
    rest = jnp.zeros((128 - table.shape[0], CH), F32)

    def body(c0):
        block = jnp.concatenate([table[:, pl.ds(c0, CH)], rest]).T
        for n, lane in enumerate(picks):
            out_ref[n, pl.ds(c0, CH), :] = jnp.broadcast_to(block[:, lane : lane + 1], (CH, 128))

    chunks(table.shape[1], body)


def first_kernel(info, own, lead1, lead2, more1, more2, anchors, demand, cost, g_out, d_out, lab_out, sums, labels, buf, sem):
    cols = own.shape[1]
    rows = 8 + 2 * FIRST
    odd = info[1]
    north_of = (odd, 1 - odd)
    loads = []
    for i in range(8):
        loads.append((own, i, FIRST + i))
    for lead, more, north in ((lead1, more1, north_of[0]), (lead2, more2, north_of[1])):
        loads.append((lead, None, FIRST + 8 - north * 9))
        for i in range(FIRST - 1):
            loads.append((more, i, (FIRST + 9) * (1 - north) + i))
    loads = [
        pltpu.make_async_copy(
            ref.at[pl.ds(0, cols), half_lanes(h)] if i is None else ref.at[i, :, half_lanes(h)],
            buf.at[at, h, pl.ds(PAD, cols), :],
            sem.at[n, h],
        )
        for n, (ref, i, at) in enumerate(loads)
        for h in range(2)
    ]
    for copy in loads:
        copy.start()
    sums[...] = jnp.zeros(sums.shape, F32)
    clear_pads(buf, rows, cols)
    for copy in loads:
        copy.wait()

    def mark(i, carry):
        node0 = (info[0] + i - FIRST) * cols

        def body(c0):
            here = pl.ds(c0 + PAD, CH)
            for h in range(2):
                buf[i, h, here, :] = anchored(buf[i, h, here, :], anchors[:, half_lanes(h)], node0 + c0)

        chunks(cols, body)
        return carry

    lax.fori_loop(0, rows, mark, 0)
    for t in range(1, STEPS + 1):
        have = rows - 2 * (t - 1)
        for side in range(2):
            at, inner = (0, 1) if side == 0 else (have - 1, have - 2)
            j = 4 * (row_of(side, t - FIRST - 1) + EDGE)

            def edge(c0, side=side, at=at, inner=inner, j=j, t=t):
                here, mid = pl.ds(c0, CH), pl.ds(c0 + PAD, CH)
                west, east, within = (cost[j + k, here, :] for k in (WEST, EAST, INNER_SIDE[side]))
                for h in range(2):
                    centre = buf[at, h, mid, :]
                    g_out[side * STEPS + t - 1, h, here, :] = jnp.minimum(
                        jnp.minimum(centre, buf[at, h, pl.ds(c0 + PAD - 1, CH), :] + west),
                        jnp.minimum(buf[at, h, pl.ds(c0 + PAD + 1, CH), :] + east, buf[inner, h, mid, :] + within),
                    )
                    d_out[side * STEPS + t - 1, h, here, :] = centre

            chunks(cols, edge)

        def row(i, carry, t=t):
            j = 4 * (i + t - FIRST + EDGE)

            def body(c0):
                here, mid = pl.ds(c0, CH), pl.ds(c0 + PAD, CH)
                west, east, up, down = (cost[j + k, here, :] for k in (WEST, EAST, NORTH, SOUTH))
                for h in range(2):
                    buf[i, h, mid, :] = jnp.minimum(
                        jnp.minimum(
                            jnp.minimum(buf[i + 1, h, mid, :], buf[i + 1, h, pl.ds(c0 + PAD - 1, CH), :] + west),
                            jnp.minimum(buf[i + 1, h, pl.ds(c0 + PAD + 1, CH), :] + east, buf[i, h, mid, :] + up),
                        ),
                        buf[i + 2, h, mid, :] + down,
                    )

            chunks(cols, body)
            return carry

        lax.fori_loop(0, have - 2, row, 0)

    done = 2 * FIRST - 4
    first_done = STEPS - FIRST
    stores = [
        pltpu.make_async_copy(
            buf.at[r, h, pl.ds(PAD, cols), :], labels.at[r + first_done, :, half_lanes(h)], sem.at[r, h]
        )
        for r in range(done)
        for h in range(2)
    ]
    for copy in stores:
        copy.start()

    def final(c0):
        for r in range(done):
            for h in range(2):
                value = buf[r, h, pl.ds(c0 + PAD, CH), :]
                for n, kept in enumerate((0, done - 1)):
                    if r == kept:
                        lab_out[n, pl.ds(c0, CH), half_lanes(h)] = value
                buf[r + done, h, pl.ds(c0 + PAD, CH), :] = jnp.exp(-temper * value)

    chunks(cols, final)

    def link(c0):
        piece = c0 // CH
        mid = pl.ds(c0 + PAD, CH)
        for r in range(done):
            inv = [demand[:, half_lanes(h)] * jnp.exp(temper * buf[r, h, mid, :]) for h in range(2)]

            def add(side, shift, other, inv=inv, r=r):
                terms = [inv[h] * buf[other + done, h, pl.ds(c0 + PAD + shift, CH), :] for h in range(2)]
                add_lane_sum(sums, side, r + first_done, piece, terms[0] + terms[1])

            add(WEST, -1, r)
            add(EAST, 1, r)
            if r > 0:
                add(NORTH, 0, r - 1)
            if r < done - 1:
                add(SOUTH, 0, r + 1)

    chunks(cols, link)
    for copy in stores:
        copy.wait()


def pick(got1, got2, odd, side, place, here, lanes):
    at = got1.shape[0] - 1 - place if side == 0 else place
    one, two = got1[at, here, lanes], got2[at, here, lanes]
    return jnp.where(odd, one, two) if side == 0 else jnp.where(odd, two, one)


def next_kernel(depth, place, last, *refs):
    info, got1, got2, anchors, demand, cost, g_in, d_in, in_lab, sums_in, _ = refs[:11]
    if last:
        far_out, lab_out, sums, labels, dbuf, ebuf, sem = refs[11:]
    else:
        g_out, d_out, lab_out, sums, labels, dbuf, ebuf, sem = refs[11:]
    cols = got1.shape[1]
    odd = info[1] > 0
    at_rows = tuple(row_of(side, STEPS - depth) for side in range(2))
    sums[...] = sums_in[...]
    stores = [pltpu.make_async_copy(lab_out.at[n], labels.at[at_rows[n]], sem.at[n]) for n in range(2)]
    clear_pads(dbuf, STEPS, cols)
    clear_pads(ebuf, 1, cols)
    for side in range(2):
        within = 0 if side == 0 else in_lab.shape[0] - 1
        node0 = (info[0] + row_of(side, -depth)) * cols

        def chain(c0, side=side, node0=node0):
            here, mid = pl.ds(c0, CH), pl.ds(c0 + PAD, CH)
            values = []
            for h in range(2):
                values.append(anchored(pick(got1, got2, odd, side, place, here, half_lanes(h)), anchors[:, half_lanes(h)], node0 + c0))
                dbuf[0, h, mid, :] = values[h]
            for t in range(1, STEPS + 1):
                outer = cost[4 * cost_row(side, t - depth) + OUTER[side], here, :]
                for h in range(2):
                    values[h] = jnp.minimum(g_in[side * STEPS + t - 1, h, here, :], values[h] + outer)
                    if t < STEPS:
                        dbuf[t, h, mid, :] = values[h]
            for h in range(2):
                lab_out[side, here, half_lanes(h)] = values[h]
                ebuf[0, h, mid, :] = jnp.exp(-temper * values[h])

        chunks(cols, chain)
        stores[side].start()

        def ahead(c0, side=side):
            here, mid = pl.ds(c0, CH), pl.ds(c0 + PAD, CH)
            best = [None, None]
            for t in range(1, STEPS + 1):
                j = 4 * cost_row(side, t - depth - 1)
                west, east, inner = (cost[j + k, here, :] for k in (WEST, EAST, INNER_SIDE[side]))
                outer = cost[j + OUTER[side], here, :] if last and t > 1 else None
                for h in range(2):
                    centre = dbuf[t - 1, h, mid, :]
                    found = jnp.minimum(
                        jnp.minimum(centre, dbuf[t - 1, h, pl.ds(c0 + PAD - 1, CH), :] + west),
                        jnp.minimum(
                            dbuf[t - 1, h, pl.ds(c0 + PAD + 1, CH), :] + east,
                            d_in[side * STEPS + t - 1, h, here, :] + inner,
                        ),
                    )
                    if not last:
                        g_out[side * STEPS + t - 1, h, here, :] = found
                        d_out[side * STEPS + t - 1, h, here, :] = centre
                    else:
                        best[h] = found if t == 1 else jnp.minimum(found, best[h] + outer)
            if last:
                for h in range(2):
                    far_out[side, h, here, :] = best[h]

        chunks(cols, ahead)

        def link(c0, side=side, within=within):
            here, mid = pl.ds(c0, CH), pl.ds(c0 + PAD, CH)
            piece = c0 // CH
            at = at_rows[side]
            inside = row_of(side, STEPS - depth + 1)
            terms = [0.0] * 4
            for h in range(2):
                dem = demand[:, half_lanes(h)]
                inv = dem * jnp.exp(temper * lab_out[side, here, half_lanes(h)])
                other = in_lab[within, here, half_lanes(h)]
                terms[0] += inv * ebuf[0, h, pl.ds(c0 + PAD - 1, CH), :]
                terms[1] += inv * ebuf[0, h, pl.ds(c0 + PAD + 1, CH), :]
                terms[2] += inv * jnp.exp(-temper * other)
                terms[3] += dem * jnp.exp(temper * other) * ebuf[0, h, mid, :]
            add_lane_sum(sums, WEST, at, piece, terms[0])
            add_lane_sum(sums, EAST, at, piece, terms[1])
            add_lane_sum(sums, INNER_SIDE[side], at, piece, terms[2])
            add_lane_sum(sums, OUTER[side], inside, piece, terms[3])

        chunks(cols, link)

    for copy in stores:
        copy.wait()


def cross_kernel(depth, info, got1, got2, anchors, demand, path, far_in, lab, sums_in, sums, sem):
    cols = got1.shape[1]
    odd = info[1] > 0
    sums[...] = sums_in[...]

    def body(c0):
        here = pl.ds(c0, CH)
        for side in range(2):
            node0 = (info[0] + row_of(side, -depth)) * cols
            terms = 0.0
            for h in range(2):
                lanes = half_lanes(h)
                value = pick(got1, got2, odd, side, 0, here, lanes)
                value = anchored(value, anchors[:, lanes], node0 + c0) + path[side, here, :]
                value = jnp.minimum(value, far_in[side, h, here, :])
                terms += demand[:, lanes] * jnp.exp(temper * (lab[side, here, lanes] - value))
            add_lane_sum(sums, OUTER[side], row_of(side, 0), c0 // CH, terms)

    chunks(cols, body)


VM = pl.BlockSpec(memory_space=pltpu.VMEM)
SM = pl.BlockSpec(memory_space=pltpu.SMEM)
HB = pl.BlockSpec(memory_space=pltpu.HBM)


def kernel_call(body, outs, scratch, limit, specs, args, aliases=None, sems=(4,)):
    return pl.pallas_call(
        body,
        out_shape=[
            jax.ShapeDtypeStruct(shape, F32) if spec is HB else pltpu.VMEM(shape, F32) for shape, spec in outs
        ],
        in_specs=specs,
        out_specs=[spec for _, spec in outs],
        scratch_shapes=[pltpu.VMEM(s, F32) for s in scratch] + [pltpu.SemaphoreType.DMA(sems)],
        compiler_params=pltpu.CompilerParams(vmem_limit_bytes=limit),
        cost_estimate=pl.CostEstimate(flops=1 << 20, bytes_accessed=32 << 20, transcendentals=0),
        input_output_aliases=aliases or {},
    )(*(pltpu.with_memory_space_constraint(v, pltpu.HBM) if spec is HB else v for v, spec in zip(args, specs)))


def local(warm, link_costs, anchor_nodes, demand):
    rows, cols, lanes = warm.shape
    count = lax.axis_size("blk")
    me = lax.axis_index("blk")
    swaps = [[(i + a, i + 1 - a) for i in range(first, count - 1, 2) for a in (0, 1)] for first in (0, 1)]
    odd = me % 2
    own = warm

    def swap(number, message):
        return lax.ppermute(message, "blk", swaps[number])

    def cut(array, number, first, size, axis):
        low, high = first - 1, rows - first - size + 1
        start = jnp.where(odd == number, high, low)
        return lax.dynamic_slice_in_dim(array, start, size, axis)

    info = jnp.stack([me * rows, odd]).astype(jnp.int32)
    flat_costs = link_costs.reshape(4 * rows, cols)
    message = ((cols + 4 * rows * cols // lanes, lanes), VM)
    lead = kernel_call(
        lead_kernel, [message] * 2, [], 1 << 20, [SM, HB, HB], (info, warm, flat_costs), sems=(2, 1 + cols // lanes)
    )
    got_lead = [swap(number, lead[number]) for number in range(2)]
    warm, lead = lax.optimization_barrier((warm, lead))

    def exchange(first, size):
        return [swap(number, cut(warm, number, first, size, 0)) for number in range(2)]

    near = [*got_lead, *exchange(2, FIRST - 1)]
    later = {k: exchange(k, SECOND if k == FIRST + 1 else 1) for k in (FIRST + 1, STEPS, STEPS + 1)}
    got_costs = [
        jnp.concatenate([m[n : n + 4 * rows] for n in range(cols, m.shape[0], 4 * rows)], axis=1) for m in got_lead
    ]
    cost_n = jnp.where(odd == 1, got_costs[0], got_costs[1]).reshape(4, rows, cols)
    cost_s = jnp.where(odd == 1, got_costs[1], got_costs[0]).reshape(4, rows, cols)

    row = (me * rows + jnp.arange(rows))[:, None]
    col = jnp.arange(cols)[None, :]
    wide = (rows, cols)
    wall = jnp.stack(
        [
            jnp.broadcast_to(col == 0, wide),
            jnp.broadcast_to(col == cols - 1, wide),
            jnp.broadcast_to(row == 0, wide),
            jnp.broadcast_to(row == rows * count - 1, wide),
        ]
    )
    own_costs = jnp.where(wall, far_value, link_costs)
    sides = ((col == 0)[None], (col == cols - 1)[None])
    cost_n, cost_s = (
        jnp.concatenate([*(jnp.where(w, far_value, c[k : k + 1]) for k, w in enumerate(sides)), c[2:]]) for c in (cost_n, cost_s)
    )
    path = jnp.stack([cost_n[NORTH, rows - EDGE :].sum(axis=0), cost_s[SOUTH, :EDGE].sum(axis=0)])
    table = jnp.concatenate([cost_n, own_costs, cost_s], axis=1).reshape(-1, cols)
    total = 3 * rows
    used = [k * total + r for r in range(rows - EDGE, 2 * rows + EDGE) for k in range(4)]
    path_wide = jnp.broadcast_to(path[:, :, None], (2, cols, 128))
    anc = anchor_nodes.reshape(1, lanes)
    dem = demand.reshape(1, lanes)
    owners = lax.axis_size("org")
    width = cols // owners
    mine = lax.dynamic_slice_in_dim(own_costs, lax.axis_index("org") * width, width, axis=2)
    scale = jnp.exp(-temper * mine) / ANCHORS
    table, path_wide, info, anc, dem, scale = lax.optimization_barrier((table, path_wide, info, anc, dem, scale))
    (cost,) = kernel_call(
        functools.partial(spread_kernel, used), [((len(used), cols, 128), VM)], [], 1 << 20, [VM], (table,)
    )
    diag = ((2 * STEPS, 2, cols, 128), VM)
    padded = cols + 2 * PAD
    pieces = ((cols // CH, 4 * rows, CH), VM)
    whole = (warm.shape, HB)
    g, d, lab, sums, labels = kernel_call(
        first_kernel,
        [diag, diag, ((2, cols, lanes), VM), pieces, whole],
        [(rows + 2 * FIRST, 2, padded, 128)],
        7680 << 10, [SM] + [HB] * 5 + [VM] * 3, (info, own, *near, anc, dem, cost),
        sems=(rows + 2 * FIRST, 2),
    )
    for place in range(SECOND):
        depth = FIRST + 1 + place
        g, d, lab, sums, labels = kernel_call(
            functools.partial(next_kernel, depth, place, False),
            [diag, diag, ((2, cols, lanes), VM), pieces, whole],
            [(STEPS, 2, padded, 128), (1, 2, padded, 128)],
            5 << 20, [SM] + [VM] * 9 + [HB],
            (info, *later[FIRST + 1], anc, dem, cost, g, d, lab, sums, labels),
            {6: 0, 7: 1, 10: 4},
        )
    far, lab, sums, labels = kernel_call(
        functools.partial(next_kernel, STEPS, 0, True),
        [((2, 2, cols, 128), VM), ((2, cols, lanes), VM), pieces, whole],
        [(STEPS, 2, padded, 128), (1, 2, padded, 128)],
        5 << 20, [SM] + [VM] * 9 + [HB], (info, *later[STEPS], anc, dem, cost, g, d, lab, sums, labels), {10: 3},
    )
    (sums,) = kernel_call(
        functools.partial(cross_kernel, STEPS + 1), [pieces], [],
        2 << 20, [SM] + [VM] * 8, (info, *later[STEPS + 1], anc, dem, path_wide, far, lab, sums),
    )
    total, bit, at = sums, 1, lax.axis_index("org")
    while bit < owners:
        pairs = total.reshape(-1, 2, 4 * rows, CH)
        mine = at // bit % 2
        keep, send = (lax.dynamic_index_in_dim(pairs, n, 1, False) for n in (mine, 1 - mine))
        total = keep + lax.ppermute(send, "org", [(i, i ^ bit) for i in range(owners)])
        bit *= 2
    return labels, total.reshape(4, rows, width) * scale


def solution(mesh):
    placed = (P("blk", None, "org"), P(None, "blk", None), P("org"), P("org"))
    return jax.shard_map(
        local,
        mesh=mesh,
        in_specs=placed,
        out_specs=(P("blk", None, "org"), P(None, "blk", "org")),
        check_vma=False,
    )
```
